32 devices in a mesh: groups: 2 (over x), gz: 16 (over z, y, core).
Axes of the slice: x: 2, y: 2, z: 4, core: 2. Of those that a mesh axis runs over, the one named last changes fastest.
Arguments:
- volume: bfloat16 [128, 64, 8, 128], P(('groups', 'gz')), parts along dimension 0, may hold values from -6 to 6
- cotangent: bfloat16 [128, 64, 8, 128], P(('groups', 'gz')), parts along dimension 0, may hold values from -6 to 6
- first_kernel: bfloat16 [27, 64, 64], replicated, may hold values from -0.15625 to 0.15625
- second_kernel: bfloat16 [27, 64, 64], replicated, may hold values from -0.15625 to 0.15625
Outputs:
- grad_volume: bfloat16 [128, 64, 8, 128], P(('groups', 'gz')), parts along dimension 0
- first_grad: float32 [54, 64, 64], P('groups'), parts along dimension 0
- second_grad: float32 [54, 64, 64], P('groups'), parts along dimension 0
The draws below stay inside these ranges and needn't reach their ends.
There are 2 independent parts, one for each index of `groups`. The reference program is written for one: setup_inputs(seed, part) draws one part's arguments, and reference() takes and returns one part's arrays. A program takes and returns all parts, laid end to end along the dimension named above; an argument that names none is the same for every part. Nothing has to cross between parts.
All inputs are finite; a program needn't handle non-finite values.
Results may differ from the reference program's by a relative error of at most 0.0031.
Values may be sent and summed in bfloat16 or wider, within the bound.
No kernel may reach another device: no remote copies, remote signals or barrier semaphores. Data moves between devices by JAX's collectives and lax.ppermute only.
A program may use at most 64 MiB of HBM per device.

```python
import math
import jax
import jax.numpy as jnp

CHANNELS = 64
ROWS = 8
COLUMNS = 128
DEPTH = 64


def shard_levels(rng, shape, cuts, low, largest):
    def one(position, shards_of):
        heights = jax.random.uniform(jax.random.fold_in(jax.random.fold_in(rng, 6), position), (shards_of,), jnp.float32, low / len(cuts), largest / len(cuts))
        return jnp.repeat(jnp.exp(heights), shape[position] // shards_of).reshape((-1,) + (1,) * (len(shape) - position - 1))

    loudness = one(*cuts[0])
    for cut in cuts[1:]:
        loudness = loudness * one(*cut)
    return loudness


def normal_values(key, shape, spread, reach, cuts=(), kind=jnp.bfloat16):
    drawn = spread * jax.random.normal(key, shape, jnp.float32)
    if cuts:
        drawn = drawn * shard_levels(key, shape, cuts, -0.22, 0.18)
    return jnp.clip(drawn, -reach, reach).astype(kind)


def setup_inputs(seed: int = 0, part: int = 0) -> dict:
    arg_keys = jax.random.split(jax.random.key(seed), 5)
    part_keys = jax.random.split(jax.random.fold_in(arg_keys[4], part), 5)
    return {
        "volume": normal_values(part_keys[0], (DEPTH, CHANNELS, ROWS, COLUMNS), 1.0, 6.0, ((0, 16),)),
        "cotangent": normal_values(part_keys[1], (DEPTH, CHANNELS, ROWS, COLUMNS), 1.0, 6.0, ((0, 16),)),
        "first_kernel": normal_values(arg_keys[2], (27, CHANNELS, CHANNELS), (27 * CHANNELS) ** -0.5, 0.15625),
        "second_kernel": normal_values(arg_keys[3], (27, CHANNELS, CHANNELS), (27 * CHANNELS) ** -0.5, 0.15625),
    }


def tap_list():
    return [(tap_d, tap_h, tap_w) for tap_d in range(3) for tap_h in range(3) for tap_w in range(3)]

def pad_grid(field):
    return jnp.pad(field, ((1, 1), (0, 0), (1, 1), (1, 1)))

def forward_conv(padded, kernel):
    layers = padded.shape[0] - 2
    height = padded.shape[2] - 2
    breadth = padded.shape[3] - 2
    summed = jnp.zeros((layers, kernel.shape[2], height, breadth), jnp.float32)
    for number, (tap_d, tap_h, tap_w) in enumerate(tap_list()):
        window = padded[tap_d:tap_d + layers, :, tap_h:tap_h + height, tap_w:tap_w + breadth].astype(jnp.float32)
        summed = summed + jnp.einsum('dchw,co->dohw', window, kernel[number].astype(jnp.float32))
    return summed

def adjoint_conv(padded, kernel):
    layers = padded.shape[0] - 2
    height = padded.shape[2] - 2
    breadth = padded.shape[3] - 2
    summed = jnp.zeros((layers, kernel.shape[1], height, breadth), jnp.float32)
    for number, (tap_d, tap_h, tap_w) in enumerate(tap_list()):
        window = padded[2 - tap_d:2 - tap_d + layers, :, 2 - tap_h:2 - tap_h + height, 2 - tap_w:2 - tap_w + breadth].astype(jnp.float32)
        summed = summed + jnp.einsum('dohw,co->dchw', window, kernel[number].astype(jnp.float32))
    return summed

def kernel_grad(padded_left, right):
    layers, unused_ch, height, breadth = right.shape
    right_f = right.astype(jnp.float32)
    pieces = []
    for tap_d, tap_h, tap_w in tap_list():
        window = padded_left[tap_d:tap_d + layers, :, tap_h:tap_h + height, tap_w:tap_w + breadth].astype(jnp.float32)
        pieces.append(jnp.einsum('dchw,dohw->co', window, right_f))
    return jnp.stack(pieces)

def reference(volume, cotangent, first_kernel, second_kernel):
    hidden = forward_conv(pad_grid(volume), first_kernel)
    sigmoid_h = jax.nn.sigmoid(hidden)
    activation = (hidden * sigmoid_h).astype(jnp.bfloat16)
    back_act = adjoint_conv(pad_grid(cotangent), second_kernel)
    grad_hidden = (back_act * sigmoid_h * (1.0 + hidden * (1.0 - sigmoid_h))).astype(jnp.bfloat16)
    grad_volume = (cotangent.astype(jnp.float32) + adjoint_conv(pad_grid(grad_hidden), first_kernel)).astype(jnp.bfloat16)
    scale_factor = 1.0 / math.sqrt(volume.shape[0] * volume.shape[2] * volume.shape[3])
    second_grad = kernel_grad(pad_grid(activation), cotangent) * scale_factor
    first_grad = kernel_grad(pad_grid(volume), grad_hidden) * scale_factor
    return (grad_volume, first_grad, second_grad)
```

```python
import functools
import math

import jax
import jax.numpy as jnp
from jax import lax
from jax.experimental import pallas as pl
from jax.experimental.pallas import tpu as pltpu
from jax.sharding import PartitionSpec as P

F32 = jnp.float32
BF16 = jnp.bfloat16
VM = pl.BlockSpec(memory_space=pltpu.VMEM)
ANY = pl.BlockSpec(memory_space=pl.ANY)
LIMIT = 24 << 20


def relayout(src, dst, wide):
    channels, rows, columns = src.shape
    wide[...] = src[...].astype(F32).reshape(channels * rows, columns)
    for row in range(rows):
        dst[:, (row + 1) * columns : (row + 2) * columns] = wide[
            pl.ds(row, channels, stride=rows), :
        ].astype(BF16)


def zero_rows(padded, columns):
    layers, channels, width = padded.shape
    zeros = jnp.zeros((channels, columns), BF16)
    for layer in range(layers):
        padded[layer, :, :columns] = zeros
        padded[layer, :, width - columns :] = zeros


def windows(three, columns, flat):
    return jnp.concatenate(
        [layer[:, b * columns : b * columns + flat] for layer in three for b in range(3)], axis=0
    )


def shifted(field, step, columns):
    channels, flat = field.shape
    lane = lax.broadcasted_iota(jnp.int32, (channels, columns), 1)
    keep = lane != (0 if step == 1 else columns - 1)
    return jnp.concatenate(
        [
            jnp.where(keep, pltpu.roll(field[:, at : at + columns], step % columns, 1), 0.0)
            for at in range(0, flat, columns)
        ],
        axis=1,
    )


def joined(three, step, columns):
    channels = three.shape[0] // 3
    return (
        three[channels : 2 * channels]
        + shifted(three[:channels], step, columns)
        + shifted(three[2 * channels :], -step, columns)
    )


def column_taps(field, step, columns):
    return jnp.concatenate(
        [
            shifted(field, -step, columns).astype(BF16),
            field.astype(BF16),
            shifted(field, step, columns).astype(BF16),
        ],
        axis=0,
    )


def one_layer(near_volume, near_cot, forward, adjoint, columns, flat):
    volume_windows = windows(near_volume, columns, flat)
    cot_windows = windows(near_cot, columns, flat)
    hidden = joined(jnp.dot(forward, volume_windows, preferred_element_type=F32), 1, columns)
    back_act = joined(jnp.dot(adjoint, cot_windows, preferred_element_type=F32), -1, columns)
    sigmoid_h = jax.nn.sigmoid(hidden)
    activation = (hidden * sigmoid_h).astype(BF16)
    grad_hidden = (back_act * sigmoid_h * (1.0 + hidden * (1.0 - sigmoid_h))).astype(BF16)
    last = (((1,), (1,)), ((), ()))
    first_term = lax.dot_general(
        volume_windows,
        column_taps(grad_hidden.astype(F32), 1, columns),
        last,
        preferred_element_type=F32,
    )
    second_term = lax.dot_general(
        column_taps(activation.astype(F32), -1, columns),
        cot_windows,
        last,
        preferred_element_type=F32,
    )
    return grad_hidden, first_term, second_term


def load_all(pairs, sems):
    copies = [pltpu.make_async_copy(src, dst, sems.at[i]) for i, (src, dst) in enumerate(pairs)]
    for copy in copies:
        copy.start()
    for copy in copies:
        copy.wait()


def inner_kernel(
    volume, cot, forward, adjoint, volume_o, cot_o, grad_o, first_o, second_o, in_v, in_c, wide, sems
):
    layers, channels, rows, columns = in_v.shape
    flat = rows * columns
    load_all([(volume, in_v), (cot, in_c)], sems)
    zero_rows(volume_o, columns)
    zero_rows(cot_o, columns)
    for layer in range(layers):
        relayout(in_v.at[layer], volume_o.at[layer], wide.at[0])
        relayout(in_c.at[layer], cot_o.at[layer], wide.at[1])
    for layer in range(1, layers - 1):
        grad_hidden, first_term, second_term = one_layer(
            [volume_o[layer + a] for a in (-1, 0, 1)],
            [cot_o[layer + a] for a in (-1, 0, 1)],
            forward[...],
            adjoint[...],
            columns,
            flat,
        )
        grad_o[layer - 1] = grad_hidden
        if layer == 1:
            first_o[...] = first_term
            second_o[...] = second_term
        else:
            first_o[...] += first_term
            second_o[...] += second_term


def pack_first(term):
    half = term.shape[0] // 2
    return term[:, :128], jnp.concatenate([term[:half, 128:], term[half:, 128:]], axis=1)


def pack_second(term):
    half = term.shape[0] // 2
    pieces = [term[:, at : at + 128] for at in range(0, 512, 128)]
    return pieces + [jnp.concatenate([term[:half, 512:], term[half:, 512:]], axis=1)]


def put_rows(dst, pieces):
    at = 0
    for piece in pieces:
        dst[at : at + piece.shape[0], :] = piece
        at += piece.shape[0]


def outer_kernel(
    before_v,
    after_v,
    before_c,
    after_c,
    volume_p,
    cot_p,
    first_in,
    second_in,
    forward,
    adjoint,
    top_o,
    bottom_o,
    mine_o,
    theirs_o,
    in_rim,
    rim_p,
    wide,
    sems,
):
    layers = volume_p.shape[0]
    unused, channels, rows, columns = in_rim.shape
    flat = rows * columns
    load_all(
        [
            (src.at[0], in_rim.at[i])
            for i, src in enumerate((before_v, after_v, before_c, after_c))
        ],
        sems,
    )
    zero_rows(rim_p, columns)
    for i in range(4):
        relayout(in_rim.at[i], rim_p.at[i], wide.at[i % 2])
    grad_top, first_top, second_top = one_layer(
        [rim_p[0], volume_p[0], volume_p[1]],
        [rim_p[2], cot_p[0], cot_p[1]],
        forward[...],
        adjoint[...],
        columns,
        flat,
    )
    top_o[0] = grad_top
    grad_bottom, first_bottom, second_bottom = one_layer(
        [volume_p[layers - 2], volume_p[layers - 1], rim_p[1]],
        [cot_p[layers - 2], cot_p[layers - 1], rim_p[3]],
        forward[...],
        adjoint[...],
        columns,
        flat,
    )
    bottom_o[0] = grad_bottom
    first = pack_first(first_in[...] + first_top + first_bottom)
    second = pack_second(second_in[...] + second_top + second_bottom)
    core = lax.axis_index("gz") % 2

    @pl.when(core == 0)
    def _():
        put_rows(mine_o, first)
        put_rows(theirs_o, second)

    @pl.when(core == 1)
    def _():
        put_rows(mine_o, second)
        put_rows(theirs_o, first)


def volume_kernel(
    before, top, inner, bottom, after, cot, adjoint, out, in_g, in_c, padded, wide, buf, sems, out_sem
):
    layers, channels, rows, columns = in_c.shape
    flat = rows * columns
    load_all(
        [
            (before.at[0], in_g.at[0]),
            (top.at[0], in_g.at[1]),
            (inner, in_g.at[pl.ds(2, layers - 2)]),
            (bottom.at[0], in_g.at[layers]),
            (after.at[0], in_g.at[layers + 1]),
            (cot, in_c),
        ],
        sems,
    )
    zero_rows(padded, columns)
    for layer in range(layers + 2):
        padded[layer, :, columns : columns + flat] = in_g[layer]
    for layer in range(layers):
        three = jnp.dot(
            adjoint[...],
            windows([padded[layer + a] for a in range(3)], columns, flat),
            preferred_element_type=F32,
        )
        summed = joined(three, -1, columns)
        scratch = wide.at[layer % 2]
        for row in range(rows):
            scratch[pl.ds(row, channels, stride=rows), :] = summed[
                :, row * columns : (row + 1) * columns
            ]
        buf[layer] = (
            in_c[layer].astype(F32) + scratch[...].reshape(channels, rows, columns)
        ).astype(BF16)
        pltpu.make_async_copy(buf.at[layer], out.at[layer], out_sem.at[layer]).start()
    for layer in range(layers):
        pltpu.make_async_copy(buf.at[layer], out.at[layer], out_sem.at[layer]).wait()


def unpack_kernel(scale, mine, other, first_o, second_o):
    channels = first_o.shape[1]

    def unpack_first(src):
        half = 9 * channels // 2
        for number in range(9):
            at = number * channels
            for c in range(2):
                first_o[3 * number + c] = (
                    src[at : at + channels, c * channels : (c + 1) * channels].astype(F32) * scale
                )
            for low in range(0, channels, channels // 2):
                row = at + low
                part, side = (row, 0) if row < half else (row - half, 1)
                first_o[3 * number + 2, low : low + channels // 2] = (
                    src[
                        9 * channels + part : 9 * channels + part + channels // 2,
                        side * channels : (side + 1) * channels,
                    ].astype(F32)
                    * scale
                )

    def unpack_second(src):
        half = 3 * channels // 2
        for number in range(9):
            for c in range(3):
                tap = 3 * (8 - number) + c
                if number < 8:
                    at = (number // 2) * 3 * channels + c * channels
                    side = number % 2
                    second_o[tap] = (
                        src[at : at + channels, side * channels : (side + 1) * channels].astype(F32)
                        * scale
                    )
                    continue
                for low in range(0, channels, channels // 2):
                    row = c * channels + low
                    part, side = (row, 0) if row < half else (row - half, 1)
                    second_o[tap, low : low + channels // 2] = (
                        src[
                            12 * channels + part : 12 * channels + part + channels // 2,
                            side * channels : (side + 1) * channels,
                        ].astype(F32)
                        * scale
                    )

    core = lax.axis_index("gz") % 2

    @pl.when(core == 0)
    def _():
        unpack_first(mine)
        unpack_second(other)

    @pl.when(core == 1)
    def _():
        unpack_first(other)
        unpack_second(mine)


def swapped(array, mask):
    return lax.ppermute(array, "gz", [(i, i ^ mask) for i in range(lax.axis_size("gz"))])


def picked(stack, i):
    return lax.dynamic_index_in_dim(stack, i, 0, keepdims=False)


def summed_over_bricks(mine, theirs):
    devices = lax.axis_size("gz")
    quarter = (lax.axis_index("gz") // 2) % 4
    stack = (mine + swapped(theirs, 1)).reshape(4, -1, *mine.shape[1:])
    total = picked(stack, quarter)
    for other in (1, 2, 3):
        sent = picked(stack, quarter ^ other).astype(BF16)
        total = total + swapped(sent, 2 * other).astype(F32)
    mask = 8
    while mask < devices:
        if devices == 16:
            total = total.astype(BF16)
        total = total.astype(F32) + swapped(total, mask).astype(F32)
        mask *= 2
    total = total.astype(BF16)
    found = jnp.stack([total] + [swapped(total, 2 * other) for other in (1, 2, 3)])
    whole = jnp.stack([picked(found, quarter ^ place) for place in range(4)])
    return whole.reshape(mine.shape)


def shards(volume, cotangent, first_kernel, second_kernel):
    layers, channels, rows, columns = volume.shape
    flat = rows * columns
    wide = flat + 2 * columns
    devices = lax.axis_size("gz")
    up = [(i, i + 1) for i in range(devices - 1)]
    down = [(j, i) for i, j in up]
    before_v = lax.ppermute(volume[layers - 1 :], "gz", up)
    before_c = lax.ppermute(cotangent[layers - 1 :], "gz", up)
    after_v = lax.ppermute(volume[:1], "gz", down)
    after_c = lax.ppermute(cotangent[:1], "gz", down)

    taps = first_kernel.reshape(3, 3, 3, channels, channels)
    forward = taps.transpose(2, 4, 0, 1, 3).reshape(3 * channels, 9 * channels)
    flipped = taps[::-1, ::-1].transpose(2, 3, 0, 1, 4).reshape(3 * channels, 9 * channels)
    taps = second_kernel.reshape(3, 3, 3, channels, channels)
    adjoint = taps[::-1, ::-1].transpose(2, 3, 0, 1, 4).reshape(3 * channels, 9 * channels)

    conv_flops = 2 * 27 * channels * channels * flat
    layer_bytes = 2 * channels * flat

    def cost(passes, moved):
        return pl.CostEstimate(
            flops=passes * conv_flops, bytes_accessed=moved * layer_bytes, transcendentals=0
        )

    def params():
        return pltpu.CompilerParams(vmem_limit_bytes=LIMIT)

    shape = jax.ShapeDtypeStruct
    volume_p, cot_p, inner, first_in, second_in = pl.pallas_call(
        inner_kernel,
        out_shape=(
            shape((layers, channels, wide), BF16),
            shape((layers, channels, wide), BF16),
            shape((layers - 2, channels, flat), BF16),
            shape((9 * channels, 3 * channels), F32),
            shape((3 * channels, 9 * channels), F32),
        ),
        in_specs=[ANY, ANY, VM, VM],
        out_specs=(VM,) * 5,
        scratch_shapes=[
            pltpu.VMEM(volume.shape, BF16),
            pltpu.VMEM(volume.shape, BF16),
            pltpu.VMEM((2, channels * rows, columns), F32),
            pltpu.SemaphoreType.DMA((2,)),
        ],
        compiler_params=params(),
        cost_estimate=cost(4 * (layers - 2), 4 * layers),
        name="inner",
    )(volume, cotangent, forward, adjoint)

    packed = shape((27 * channels * channels // 128, 128), F32)
    top, bottom, mine, theirs = pl.pallas_call(
        outer_kernel,
        out_shape=(shape((1, channels, flat), BF16),) * 2 + (packed,) * 2,
        in_specs=[ANY] * 4 + [VM] * 6,
        out_specs=(VM,) * 4,
        scratch_shapes=[
            pltpu.VMEM((4, channels, rows, columns), BF16),
            pltpu.VMEM((4, channels, wide), BF16),
            pltpu.VMEM((2, channels * rows, columns), F32),
            pltpu.SemaphoreType.DMA((4,)),
        ],
        compiler_params=params(),
        cost_estimate=cost(8, 16),
        name="outer",
    )(before_v, after_v, before_c, after_c, volume_p, cot_p, first_in, second_in, forward, adjoint)

    before_g = lax.ppermute(bottom, "gz", up)
    after_g = lax.ppermute(top, "gz", down)
    grad_volume = pl.pallas_call(
        volume_kernel,
        out_shape=shape(volume.shape, BF16),
        in_specs=[ANY] * 6 + [VM],
        out_specs=ANY,
        scratch_shapes=[
            pltpu.VMEM((layers + 2, channels, flat), BF16),
            pltpu.VMEM(volume.shape, BF16),
            pltpu.VMEM((layers + 2, channels, wide), BF16),
            pltpu.VMEM((2, channels * rows, columns), F32),
            pltpu.VMEM(volume.shape, BF16),
            pltpu.SemaphoreType.DMA((6,)),
            pltpu.SemaphoreType.DMA((layers,)),
        ],
        compiler_params=params(),
        cost_estimate=cost(layers, 4 * layers),
        name="volume",
    )(before_g, top, inner, bottom, after_g, cotangent, flipped)

    tiles = (packed.shape[0] // 8, 8, 128)
    own = summed_over_bricks(mine.reshape(tiles), theirs.reshape(tiles))
    other = swapped(own, 1)
    scale = 1.0 / math.sqrt(layers * devices * flat)
    first_grad, second_grad = pl.pallas_call(
        functools.partial(unpack_kernel, scale),
        out_shape=(shape((27, channels, channels), F32),) * 2,
        in_specs=[VM] * 2,
        out_specs=(VM,) * 2,
        compiler_params=params(),
        cost_estimate=cost(0, 10),
        name="unpack",
    )(own.reshape(packed.shape), other.reshape(packed.shape))
    return grad_volume, first_grad, second_grad


def solution(mesh):
    placed = (
        P(("groups", "gz"), None, None, None),
        P(("groups", "gz"), None, None, None),
        P(),
        P(),
    )
    return jax.shard_map(
        shards,
        mesh=mesh,
        in_specs=placed,
        out_specs=(
            P(("groups", "gz"), None, None, None),
            P("groups", None, None),
            P("groups", None, None),
        ),
        check_vma=False,
    )
```

```python
import functools
import math

import jax
import jax.numpy as jnp
from jax import lax
from jax.experimental import pallas as pl
from jax.experimental.pallas import tpu as pltpu
from jax.sharding import PartitionSpec as P

F32 = jnp.float32
BF16 = jnp.bfloat16
VM = pl.BlockSpec(memory_space=pltpu.VMEM)
ANY = pl.BlockSpec(memory_space=pl.ANY)
LIMIT = 24 << 20


def relayout(src, dst, wide):
    channels, rows, columns = src.shape
    wide[...] = src[...].astype(F32).reshape(channels * rows, columns)
    for row in range(rows):
        dst[:, (row + 1) * columns : (row + 2) * columns] = wide[
            pl.ds(row, channels, stride=rows), :
        ].astype(BF16)


def zero_rows(padded, columns):
    layers, channels, width = padded.shape
    zeros = jnp.zeros((channels, columns), BF16)
    for layer in range(layers):
        padded[layer, :, :columns] = zeros
        padded[layer, :, width - columns :] = zeros


def windows(three, columns, flat):
    return jnp.concatenate(
        [layer[:, b * columns : b * columns + flat] for layer in three for b in range(3)], axis=0
    )


def shifted(field, step, columns):
    channels, flat = field.shape
    lane = lax.broadcasted_iota(jnp.int32, (channels, columns), 1)
    keep = lane != (0 if step == 1 else columns - 1)
    return jnp.concatenate(
        [
            jnp.where(keep, pltpu.roll(field[:, at : at + columns], step % columns, 1), 0.0)
            for at in range(0, flat, columns)
        ],
        axis=1,
    )


def joined(three, step, columns):
    channels = three.shape[0] // 3
    return (
        three[channels : 2 * channels]
        + shifted(three[:channels], step, columns)
        + shifted(three[2 * channels :], -step, columns)
    )


def column_taps(field, step, columns):
    return jnp.concatenate(
        [
            shifted(field, -step, columns).astype(BF16),
            field.astype(BF16),
            shifted(field, step, columns).astype(BF16),
        ],
        axis=0,
    )


def one_layer(near_volume, near_cot, forward, adjoint, columns, flat):
    volume_windows = windows(near_volume, columns, flat)
    cot_windows = windows(near_cot, columns, flat)
    hidden = joined(jnp.dot(forward, volume_windows, preferred_element_type=F32), 1, columns)
    back_act = joined(jnp.dot(adjoint, cot_windows, preferred_element_type=F32), -1, columns)
    sigmoid_h = jax.nn.sigmoid(hidden)
    activation = (hidden * sigmoid_h).astype(BF16)
    grad_hidden = (back_act * sigmoid_h * (1.0 + hidden * (1.0 - sigmoid_h))).astype(BF16)
    last = (((1,), (1,)), ((), ()))
    first_term = lax.dot_general(
        volume_windows,
        column_taps(grad_hidden.astype(F32), 1, columns),
        last,
        preferred_element_type=F32,
    )
    second_term = lax.dot_general(
        column_taps(activation.astype(F32), -1, columns),
        cot_windows,
        last,
        preferred_element_type=F32,
    )
    return grad_hidden, first_term, second_term


def load_all(pairs, sems):
    copies = [pltpu.make_async_copy(src, dst, sems.at[i]) for i, (src, dst) in enumerate(pairs)]
    for copy in copies:
        copy.start()
    for copy in copies:
        copy.wait()


def forward_taps(taps, out):
    for number in range(9):
        channels = taps.shape[1]
        row = jnp.concatenate([taps[3 * number + c].astype(F32) for c in range(3)], axis=1)
        out[:, number * channels : (number + 1) * channels] = row.T.astype(BF16)


def adjoint_taps(taps, out):
    channels = taps.shape[1]
    for c in range(3):
        out[c * channels : (c + 1) * channels, :] = jnp.concatenate(
            [taps[3 * (8 - number) + c] for number in range(9)], axis=1
        )


def inner_kernel(
    volume,
    cot,
    first_k,
    second_k,
    volume_o,
    cot_o,
    grad_o,
    first_o,
    second_o,
    forward,
    adjoint,
    flipped,
    in_v,
    in_c,
    in_k,
    wide,
    sems,
):
    layers, channels, rows, columns = in_v.shape
    flat = rows * columns
    load_all(
        [(first_k, in_k.at[0]), (second_k, in_k.at[1]), (volume, in_v), (cot, in_c)], sems
    )
    forward_taps(in_k.at[0], forward)
    adjoint_taps(in_k.at[1], adjoint)
    adjoint_taps(in_k.at[0], flipped)
    zero_rows(volume_o, columns)
    zero_rows(cot_o, columns)
    for layer in range(layers):
        relayout(in_v.at[layer], volume_o.at[layer], wide.at[0])
        relayout(in_c.at[layer], cot_o.at[layer], wide.at[1])
    for layer in range(1, layers - 1):
        grad_hidden, first_term, second_term = one_layer(
            [volume_o[layer + a] for a in (-1, 0, 1)],
            [cot_o[layer + a] for a in (-1, 0, 1)],
            forward[...],
            adjoint[...],
            columns,
            flat,
        )
        grad_o[layer - 1] = grad_hidden
        if layer == 1:
            first_o[...] = first_term
            second_o[...] = second_term
        else:
            first_o[...] += first_term
            second_o[...] += second_term


def pack_first(term):
    half = term.shape[0] // 2
    return term[:, :128], jnp.concatenate([term[:half, 128:], term[half:, 128:]], axis=1)


def pack_second(term):
    half = term.shape[0] // 2
    pieces = [term[:, at : at + 128] for at in range(0, 512, 128)]
    return pieces + [jnp.concatenate([term[:half, 512:], term[half:, 512:]], axis=1)]


def put_rows(dst, pieces):
    at = 0
    for piece in pieces:
        dst[at : at + piece.shape[0], :] = piece
        at += piece.shape[0]


def outer_kernel(
    before,
    after,
    volume_p,
    cot_p,
    first_in,
    second_in,
    forward,
    adjoint,
    top_o,
    bottom_o,
    mine_o,
    theirs_o,
    in_rim,
    rim_p,
    wide,
    sems,
):
    layers = volume_p.shape[0]
    unused, channels, rows, columns = in_rim.shape
    flat = rows * columns
    load_all(
        [
            (src.at[0, pl.ds(kind * channels, channels)], in_rim.at[2 * kind + i])
            for kind in range(2)
            for i, src in enumerate((before, after))
        ],
        sems,
    )
    zero_rows(rim_p, columns)
    for i in range(4):
        relayout(in_rim.at[i], rim_p.at[i], wide.at[i % 2])
    grad_top, first_top, second_top = one_layer(
        [rim_p[0], volume_p[0], volume_p[1]],
        [rim_p[2], cot_p[0], cot_p[1]],
        forward[...],
        adjoint[...],
        columns,
        flat,
    )
    top_o[0] = grad_top
    grad_bottom, first_bottom, second_bottom = one_layer(
        [volume_p[layers - 2], volume_p[layers - 1], rim_p[1]],
        [cot_p[layers - 2], cot_p[layers - 1], rim_p[3]],
        forward[...],
        adjoint[...],
        columns,
        flat,
    )
    bottom_o[0] = grad_bottom
    first = pack_first(first_in[...] + first_top + first_bottom)
    second = pack_second(second_in[...] + second_top + second_bottom)
    core = lax.axis_index("gz") & 1

    @pl.when(core == 0)
    def _():
        put_rows(mine_o, first)
        put_rows(theirs_o, second)

    @pl.when(core == 1)
    def _():
        put_rows(mine_o, second)
        put_rows(theirs_o, first)


def volume_kernel(
    before, top, inner, bottom, after, cot, adjoint, out, in_g, in_c, padded, wide, buf, sems, out_sem
):
    layers, channels, rows, columns = in_c.shape
    flat = rows * columns
    load_all(
        [
            (before.at[0], in_g.at[0]),
            (top.at[0], in_g.at[1]),
            (inner, in_g.at[pl.ds(2, layers - 2)]),
            (bottom.at[0], in_g.at[layers]),
            (after.at[0], in_g.at[layers + 1]),
            (cot, in_c),
        ],
        sems,
    )
    zero_rows(padded, columns)
    for layer in range(layers + 2):
        padded[layer, :, columns : columns + flat] = in_g[layer]
    for layer in range(layers):
        three = jnp.dot(
            adjoint[...],
            windows([padded[layer + a] for a in range(3)], columns, flat),
            preferred_element_type=F32,
        )
        summed = joined(three, -1, columns)
        scratch = wide.at[layer % 2]
        for row in range(rows):
            scratch[pl.ds(row, channels, stride=rows), :] = summed[
                :, row * columns : (row + 1) * columns
            ]
        buf[layer] = (
            in_c[layer].astype(F32) + scratch[...].reshape(channels, rows, columns)
        ).astype(BF16)
        pltpu.make_async_copy(buf.at[layer], out.at[layer], out_sem.at[layer]).start()
    for layer in range(layers):
        pltpu.make_async_copy(buf.at[layer], out.at[layer], out_sem.at[layer]).wait()


def unpack_kernel(scale, mine, other, first_o, second_o):
    channels = first_o.shape[1]

    def unpack_first(src):
        half = 9 * channels // 2
        for number in range(9):
            at = number * channels
            for c in range(2):
                first_o[3 * number + c] = (
                    src[at : at + channels, c * channels : (c + 1) * channels].astype(F32) * scale
                )
            for low in range(0, channels, channels // 2):
                row = at + low
                part, side = (row, 0) if row < half else (row - half, 1)
                first_o[3 * number + 2, low : low + channels // 2] = (
                    src[
                        9 * channels + part : 9 * channels + part + channels // 2,
                        side * channels : (side + 1) * channels,
                    ].astype(F32)
                    * scale
                )

    def unpack_second(src):
        half = 3 * channels // 2
        for number in range(9):
            for c in range(3):
                tap = 3 * (8 - number) + c
                if number < 8:
                    at = (number // 2) * 3 * channels + c * channels
                    side = number % 2
                    second_o[tap] = (
                        src[at : at + channels, side * channels : (side + 1) * channels].astype(F32)
                        * scale
                    )
                    continue
                for low in range(0, channels, channels // 2):
                    row = c * channels + low
                    part, side = (row, 0) if row < half else (row - half, 1)
                    second_o[tap, low : low + channels // 2] = (
                        src[
                            12 * channels + part : 12 * channels + part + channels // 2,
                            side * channels : (side + 1) * channels,
                        ].astype(F32)
                        * scale
                    )

    core = lax.axis_index("gz") & 1

    @pl.when(core == 0)
    def _():
        unpack_first(mine)
        unpack_second(other)

    @pl.when(core == 1)
    def _():
        unpack_first(other)
        unpack_second(mine)


def swapped(array, mask):
    return lax.ppermute(array, "gz", [(i, i ^ mask) for i in range(lax.axis_size("gz"))])


def picked(stack, i):
    return lax.dynamic_index_in_dim(stack, i, 0, keepdims=False)


def quarter_of(mine, theirs):
    quarter = (lax.axis_index("gz") >> 1) & 3
    stack = (mine + swapped(theirs, 1)).reshape(4, -1, *mine.shape[1:])
    sent = [picked(stack, quarter ^ other).astype(BF16) for other in (1, 2, 3)]
    return picked(stack, quarter), sent


def whole_sum(terms, shape):
    quarter = (lax.axis_index("gz") >> 1) & 3
    total = sum(term.astype(F32) for term in terms)
    mask = 8
    while mask < lax.axis_size("gz"):
        total = total + swapped(total, mask)
        mask *= 2
    total = total.astype(BF16)
    found = jnp.stack([total] + [swapped(total, 2 * other) for other in (1, 2, 3)])
    whole = jnp.stack([picked(found, quarter ^ place) for place in range(4)])
    return whole.reshape(shape)


def shards(volume, cotangent, first_kernel, second_kernel):
    layers, channels, rows, columns = volume.shape
    flat = rows * columns
    wide = flat + 2 * columns
    devices = lax.axis_size("gz")
    up = [(i, i + 1) for i in range(devices - 1)]
    down = [(j, i) for i, j in up]
    last = jnp.concatenate([volume[layers - 1 :], cotangent[layers - 1 :]], axis=1)
    first = jnp.concatenate([volume[:1], cotangent[:1]], axis=1)
    before = lax.ppermute(last, "gz", up)
    after = lax.ppermute(first, "gz", down)

    conv_flops = 2 * 27 * channels * channels * flat
    layer_bytes = 2 * channels * flat

    def cost(passes, moved):
        return pl.CostEstimate(
            flops=passes * conv_flops, bytes_accessed=moved * layer_bytes, transcendentals=0
        )

    def params():
        return pltpu.CompilerParams(vmem_limit_bytes=LIMIT)

    shape = jax.ShapeDtypeStruct
    taps = shape((3 * channels, 9 * channels), BF16)
    volume_p, cot_p, inner, first_in, second_in, forward, adjoint, flipped = pl.pallas_call(
        inner_kernel,
        out_shape=(
            shape((layers, channels, wide), BF16),
            shape((layers, channels, wide), BF16),
            shape((layers - 2, channels, flat), BF16),
            shape((9 * channels, 3 * channels), F32),
            shape((3 * channels, 9 * channels), F32),
            taps,
            taps,
            taps,
        ),
        in_specs=[ANY] * 4,
        out_specs=(VM,) * 8,
        scratch_shapes=[
            pltpu.VMEM(volume.shape, BF16),
            pltpu.VMEM(volume.shape, BF16),
            pltpu.VMEM((2, 27, channels, channels), BF16),
            pltpu.VMEM((2, channels * rows, columns), F32),
            pltpu.SemaphoreType.DMA((4,)),
        ],
        compiler_params=params(),
        cost_estimate=cost(4 * (layers - 2), 4 * layers),
        name="inner",
    )(volume, cotangent, first_kernel, second_kernel)

    packed = shape((27 * channels * channels // 128, 128), F32)
    top, bottom, mine, theirs = pl.pallas_call(
        outer_kernel,
        out_shape=(shape((1, channels, flat), BF16),) * 2 + (packed,) * 2,
        in_specs=[ANY] * 2 + [VM] * 6,
        out_specs=(VM,) * 4,
        scratch_shapes=[
            pltpu.VMEM((4, channels, rows, columns), BF16),
            pltpu.VMEM((4, channels, wide), BF16),
            pltpu.VMEM((2, channels * rows, columns), F32),
            pltpu.SemaphoreType.DMA((4,)),
        ],
        compiler_params=params(),
        cost_estimate=cost(8, 16),
        name="outer",
    )(before, after, volume_p, cot_p, first_in, second_in, forward, adjoint)

    tiles = (packed.shape[0] // 8, 8, 128)
    before_g = lax.ppermute(bottom, "gz", up)
    after_g = lax.ppermute(top, "gz", down)
    own, sent = quarter_of(mine.reshape(tiles), theirs.reshape(tiles))
    sent, flipped = lax.optimization_barrier((sent, flipped))
    terms = [own] + [swapped(sent[other - 1], 2 * other) for other in (1, 2, 3)]
    grad_volume = pl.pallas_call(
        volume_kernel,
        out_shape=shape(volume.shape, BF16),
        in_specs=[ANY] * 6 + [VM],
        out_specs=ANY,
        scratch_shapes=[
            pltpu.VMEM((layers + 2, channels, flat), BF16),
            pltpu.VMEM(volume.shape, BF16),
            pltpu.VMEM((layers + 2, channels, wide), BF16),
            pltpu.VMEM((2, channels * rows, columns), F32),
            pltpu.VMEM(volume.shape, BF16),
            pltpu.SemaphoreType.DMA((6,)),
            pltpu.SemaphoreType.DMA((layers,)),
        ],
        compiler_params=params(),
        cost_estimate=cost(layers, 4 * layers),
        name="volume",
    )(before_g, top, inner, bottom, after_g, cotangent, flipped)

    terms, grad_volume = lax.optimization_barrier((terms, grad_volume))
    own = whole_sum(terms, tiles)
    other = swapped(own, 1)
    scale = 1.0 / math.sqrt(layers * devices * flat)
    first_grad, second_grad = pl.pallas_call(
        functools.partial(unpack_kernel, scale),
        out_shape=(shape((27, channels, channels), F32),) * 2,
        in_specs=[VM] * 2,
        out_specs=(VM,) * 2,
        compiler_params=params(),
        cost_estimate=cost(0, 10),
        name="unpack",
    )(own.reshape(packed.shape), other.reshape(packed.shape))
    return grad_volume, first_grad, second_grad


def solution(mesh):
    placed = (
        P(("groups", "gz"), None, None, None),
        P(("groups", "gz"), None, None, None),
        P(),
        P(),
    )
    return jax.shard_map(
        shards,
        mesh=mesh,
        in_specs=placed,
        out_specs=(
            P(("groups", "gz"), None, None, None),
            P("groups", None, None),
            P("groups", None, None),
        ),
        check_vma=False,
    )
```

```python
import functools
import math

import jax
import jax.numpy as jnp
from jax import lax
from jax.experimental import pallas as pl
from jax.experimental.pallas import tpu as pltpu
from jax.sharding import PartitionSpec as P

F32 = jnp.float32
BF16 = jnp.bfloat16
VM = pl.BlockSpec(memory_space=pltpu.VMEM)
ANY = pl.BlockSpec(memory_space=pl.ANY)
LIMIT = 24 << 20


def relayout(src, dst, wide):
    channels, rows, columns = src.shape
    wide[...] = src[...].astype(F32).reshape(channels * rows, columns)
    for row in range(rows):
        dst[:, (row + 1) * columns : (row + 2) * columns] = wide[
            pl.ds(row, channels, stride=rows), :
        ].astype(BF16)


def zero_rows(padded, columns):
    layers, channels, width = padded.shape
    zeros = jnp.zeros((channels, columns), BF16)
    for layer in range(layers):
        padded[layer, :, :columns] = zeros
        padded[layer, :, width - columns :] = zeros


def windows(three, columns, flat):
    return jnp.concatenate(
        [layer[:, b * columns : b * columns + flat] for layer in three for b in range(3)], axis=0
    )


def shifted(field, step, columns):
    channels, flat = field.shape
    lane = lax.broadcasted_iota(jnp.int32, (channels, columns), 1)
    keep = lane != (0 if step == 1 else columns - 1)
    return jnp.concatenate(
        [
            jnp.where(keep, pltpu.roll(field[:, at : at + columns], step % columns, 1), 0.0)
            for at in range(0, flat, columns)
        ],
        axis=1,
    )


def joined(three, step, columns):
    channels = three.shape[0] // 3
    return (
        three[channels : 2 * channels]
        + shifted(three[:channels], step, columns)
        + shifted(three[2 * channels :], -step, columns)
    )


def column_taps(field, step, columns):
    return jnp.concatenate(
        [
            shifted(field, -step, columns).astype(BF16),
            field.astype(BF16),
            shifted(field, step, columns).astype(BF16),
        ],
        axis=0,
    )


def one_layer(near_volume, near_cot, forward, adjoint, columns, flat):
    volume_windows = windows(near_volume, columns, flat)
    cot_windows = windows(near_cot, columns, flat)
    hidden = joined(jnp.dot(forward, volume_windows, preferred_element_type=F32), 1, columns)
    back_act = joined(jnp.dot(adjoint, cot_windows, preferred_element_type=F32), -1, columns)
    sigmoid_h = jax.nn.sigmoid(hidden)
    activation = (hidden * sigmoid_h).astype(BF16)
    grad_hidden = (back_act * sigmoid_h * (1.0 + hidden * (1.0 - sigmoid_h))).astype(BF16)
    last = (((1,), (1,)), ((), ()))
    first_term = lax.dot_general(
        volume_windows,
        column_taps(grad_hidden.astype(F32), 1, columns),
        last,
        preferred_element_type=F32,
    )
    second_term = lax.dot_general(
        column_taps(activation.astype(F32), -1, columns),
        cot_windows,
        last,
        preferred_element_type=F32,
    )
    return grad_hidden, first_term, second_term


def forward_taps(taps, out):
    for number in range(9):
        channels = taps.shape[1]
        row = jnp.concatenate([taps[3 * number + c].astype(F32) for c in range(3)], axis=1)
        out[:, number * channels : (number + 1) * channels] = row.T.astype(BF16)


def adjoint_taps(taps, out):
    channels = taps.shape[1]
    for c in range(3):
        out[c * channels : (c + 1) * channels, :] = jnp.concatenate(
            [taps[3 * (8 - number) + c] for number in range(9)], axis=1
        )


def inner_kernel(
    volume,
    cot,
    first_k,
    second_k,
    volume_o,
    cot_o,
    grad_o,
    first_o,
    second_o,
    forward,
    adjoint,
    flipped,
    wide,
):
    layers, channels, rows, columns = volume.shape
    flat = rows * columns
    forward_taps(first_k, forward)
    adjoint_taps(second_k, adjoint)
    adjoint_taps(first_k, flipped)
    zero_rows(volume_o, columns)
    zero_rows(cot_o, columns)
    for layer in range(layers):
        relayout(volume.at[layer], volume_o.at[layer], wide.at[0])
        relayout(cot.at[layer], cot_o.at[layer], wide.at[1])
    for layer in range(1, layers - 1):
        grad_hidden, first_term, second_term = one_layer(
            [volume_o[layer + a] for a in (-1, 0, 1)],
            [cot_o[layer + a] for a in (-1, 0, 1)],
            forward[...],
            adjoint[...],
            columns,
            flat,
        )
        grad_o[layer - 1] = grad_hidden
        if layer == 1:
            first_o[...] = first_term
            second_o[...] = second_term
        else:
            first_o[...] += first_term
            second_o[...] += second_term


def pack_first(term):
    half = term.shape[0] // 2
    return term[:, :128], jnp.concatenate([term[:half, 128:], term[half:, 128:]], axis=1)


def pack_second(term):
    half = term.shape[0] // 2
    pieces = [term[:, at : at + 128] for at in range(0, 512, 128)]
    return pieces + [jnp.concatenate([term[:half, 512:], term[half:, 512:]], axis=1)]


def put_rows(dst, pieces):
    at = 0
    for piece in pieces:
        dst[at : at + piece.shape[0], :] = piece
        at += piece.shape[0]


def outer_kernel(
    on_chip,
    off_chip,
    volume_p,
    cot_p,
    first_in,
    second_in,
    forward,
    adjoint,
    top_o,
    bottom_o,
    mine_o,
    theirs_o,
    rim_p,
    wide,
):
    layers = volume_p.shape[0]
    channels = on_chip.shape[1] // 2
    rows, columns = on_chip.shape[2:]
    flat = rows * columns
    core = lax.axis_index("gz") & 1
    zero_rows(rim_p, columns)
    for kind in range(2):
        part = pl.ds(kind * channels, channels)
        relayout(on_chip.at[0, part], rim_p.at[2 * kind + 1 - core], wide.at[0])
        relayout(off_chip.at[0, part], rim_p.at[2 * kind + core], wide.at[1])
    grad_top, first_top, second_top = one_layer(
        [rim_p[0], volume_p[0], volume_p[1]],
        [rim_p[2], cot_p[0], cot_p[1]],
        forward[...],
        adjoint[...],
        columns,
        flat,
    )
    top_o[0] = grad_top
    grad_bottom, first_bottom, second_bottom = one_layer(
        [volume_p[layers - 2], volume_p[layers - 1], rim_p[1]],
        [cot_p[layers - 2], cot_p[layers - 1], rim_p[3]],
        forward[...],
        adjoint[...],
        columns,
        flat,
    )
    bottom_o[0] = grad_bottom
    first = pack_first(first_in[...] + first_top + first_bottom)
    second = pack_second(second_in[...] + second_top + second_bottom)

    @pl.when(core == 0)
    def _():
        put_rows(mine_o, first)
        put_rows(theirs_o, second)

    @pl.when(core == 1)
    def _():
        put_rows(mine_o, second)
        put_rows(theirs_o, first)


def volume_kernel(
    on_chip, off_chip, top, inner, bottom, cot, adjoint, out, padded, wide, buf, out_sem
):
    layers, channels, rows, columns = cot.shape
    flat = rows * columns
    core = lax.axis_index("gz") & 1
    zero_rows(padded, columns)
    middle = slice(columns, columns + flat)
    padded[(1 - core) * (layers + 1), :, middle] = on_chip[0]
    padded[core * (layers + 1), :, middle] = off_chip[0]
    padded[1, :, middle] = top[0]
    padded[layers, :, middle] = bottom[0]
    for layer in range(layers - 2):
        padded[layer + 2, :, middle] = inner[layer]
    for layer in range(layers):
        three = jnp.dot(
            adjoint[...],
            windows([padded[layer + a] for a in range(3)], columns, flat),
            preferred_element_type=F32,
        )
        summed = joined(three, -1, columns)
        scratch = wide.at[layer % 2]
        for row in range(rows):
            scratch[pl.ds(row, channels, stride=rows), :] = summed[
                :, row * columns : (row + 1) * columns
            ]
        buf[layer] = (
            cot[layer].astype(F32) + scratch[...].reshape(channels, rows, columns)
        ).astype(BF16)
        pltpu.make_async_copy(buf.at[layer], out.at[layer], out_sem.at[layer]).start()
    for layer in range(layers):
        pltpu.make_async_copy(buf.at[layer], out.at[layer], out_sem.at[layer]).wait()


def unpack_kernel(scale, mine, other, first_o, second_o):
    channels = first_o.shape[1]

    def unpack_first(src):
        half = 9 * channels // 2
        for number in range(9):
            at = number * channels
            for c in range(2):
                first_o[3 * number + c] = (
                    src[at : at + channels, c * channels : (c + 1) * channels].astype(F32) * scale
                )
            for low in range(0, channels, channels // 2):
                row = at + low
                part, side = (row, 0) if row < half else (row - half, 1)
                first_o[3 * number + 2, low : low + channels // 2] = (
                    src[
                        9 * channels + part : 9 * channels + part + channels // 2,
                        side * channels : (side + 1) * channels,
                    ].astype(F32)
                    * scale
                )

    def unpack_second(src):
        half = 3 * channels // 2
        for number in range(9):
            for c in range(3):
                tap = 3 * (8 - number) + c
                if number < 8:
                    at = (number // 2) * 3 * channels + c * channels
                    side = number % 2
                    second_o[tap] = (
                        src[at : at + channels, side * channels : (side + 1) * channels].astype(F32)
                        * scale
                    )
                    continue
                for low in range(0, channels, channels // 2):
                    row = c * channels + low
                    part, side = (row, 0) if row < half else (row - half, 1)
                    second_o[tap, low : low + channels // 2] = (
                        src[
                            12 * channels + part : 12 * channels + part + channels // 2,
                            side * channels : (side + 1) * channels,
                        ].astype(F32)
                        * scale
                    )

    core = lax.axis_index("gz") & 1

    @pl.when(core == 0)
    def _():
        unpack_first(mine)
        unpack_second(other)

    @pl.when(core == 1)
    def _():
        unpack_first(other)
        unpack_second(mine)


def swapped(array, mask):
    return lax.ppermute(array, "gz", [(i, i ^ mask) for i in range(lax.axis_size("gz"))])


def swapped_chips(array):
    pairs = [(i, i + 1) for i in range(1, lax.axis_size("gz") - 1, 2)]
    return lax.ppermute(array, "gz", pairs + [(j, i) for i, j in pairs])


def picked(stack, i):
    return lax.dynamic_index_in_dim(stack, i, 0, keepdims=False)


def quarter_of(mine, theirs):
    quarter = (lax.axis_index("gz") >> 1) & 3
    stack = (mine + swapped(theirs, 1)).reshape(4, -1, *mine.shape[1:])
    sent = [picked(stack, quarter ^ other).astype(BF16) for other in (1, 2, 3)]
    return picked(stack, quarter), sent


def whole_sum(total, shape):
    quarter = (lax.axis_index("gz") >> 1) & 3
    mask = 16
    while mask < lax.axis_size("gz"):
        total = total + swapped(total, mask)
        mask *= 2
    total = total.astype(BF16)
    found = jnp.stack([total] + [swapped(total, 2 * other) for other in (1, 2, 3)])
    whole = jnp.stack([picked(found, quarter ^ place) for place in range(4)])
    return whole.reshape(shape)


def shards(volume, cotangent, first_kernel, second_kernel):
    layers, channels, rows, columns = volume.shape
    flat = rows * columns
    wide = flat + 2 * columns
    devices = lax.axis_size("gz")
    core = lax.axis_index("gz") & 1
    edge = jnp.where(core == 0, layers - 1, 0)
    other_edge = layers - 1 - edge
    near = [jnp.concatenate([lax.dynamic_slice_in_dim(x, at, 1) for x in (volume, cotangent)], axis=1) for at in (edge, other_edge)]
    on_chip, off_chip = swapped(near[0], 1), swapped_chips(near[1])

    conv_flops = 2 * 27 * channels * channels * flat
    layer_bytes = 2 * channels * flat

    def cost(passes, moved):
        return pl.CostEstimate(
            flops=passes * conv_flops, bytes_accessed=moved * layer_bytes, transcendentals=0
        )

    def params():
        return pltpu.CompilerParams(vmem_limit_bytes=LIMIT)

    shape = jax.ShapeDtypeStruct
    taps = shape((3 * channels, 9 * channels), BF16)
    volume_p, cot_p, inner, first_in, second_in, forward, adjoint, flipped = pl.pallas_call(
        inner_kernel,
        out_shape=(
            shape((layers, channels, wide), BF16),
            shape((layers, channels, wide), BF16),
            shape((layers - 2, channels, flat), BF16),
            shape((9 * channels, 3 * channels), F32),
            shape((3 * channels, 9 * channels), F32),
            taps,
            taps,
            taps,
        ),
        in_specs=[VM] * 4,
        out_specs=(VM,) * 8,
        scratch_shapes=[pltpu.VMEM((2, channels * rows, columns), F32)],
        compiler_params=params(),
        cost_estimate=cost(4 * (layers - 2), 4 * layers),
        name="inner",
    )(volume, cotangent, first_kernel, second_kernel)

    packed = shape((27 * channels * channels // 128, 128), F32)
    top, bottom, mine, theirs = pl.pallas_call(
        outer_kernel,
        out_shape=(shape((1, channels, flat), BF16),) * 2 + (packed,) * 2,
        in_specs=[VM] * 8,
        out_specs=(VM,) * 4,
        scratch_shapes=[
            pltpu.VMEM((4, channels, wide), BF16),
            pltpu.VMEM((2, channels * rows, columns), F32),
        ],
        compiler_params=params(),
        cost_estimate=cost(8, 16),
        name="outer",
    )(on_chip, off_chip, volume_p, cot_p, first_in, second_in, forward, adjoint)

    tiles = (packed.shape[0] // 8, 8, 128)
    own, sent = quarter_of(mine.reshape(tiles), theirs.reshape(tiles))
    sent, top, bottom = lax.optimization_barrier((sent, top, bottom))
    terms = [own] + [swapped(sent[other - 1], 2 * other) for other in (1, 2, 3)]
    on_chip_g = swapped(jnp.where(core == 0, bottom, top), 1)
    off_chip_g = swapped_chips(jnp.where(core == 0, top, bottom))
    total = sum(term.astype(F32) for term in terms)
    total, flipped = lax.optimization_barrier((total, flipped))
    further = swapped(total, 8)
    grad_volume = pl.pallas_call(
        volume_kernel,
        out_shape=shape(volume.shape, BF16),
        in_specs=[VM] * 7,
        out_specs=ANY,
        scratch_shapes=[
            pltpu.VMEM((layers + 2, channels, wide), BF16),
            pltpu.VMEM((2, channels * rows, columns), F32),
            pltpu.VMEM(volume.shape, BF16),
            pltpu.SemaphoreType.DMA((layers,)),
        ],
        compiler_params=params(),
        cost_estimate=cost(layers, 4 * layers),
        name="volume",
    )(on_chip_g, off_chip_g, top, inner, bottom, cotangent, flipped)

    further, grad_volume = lax.optimization_barrier((further, grad_volume))
    own = whole_sum(total + further, tiles)
    other = swapped(own, 1)
    scale = 1.0 / math.sqrt(layers * devices * flat)
    first_grad, second_grad = pl.pallas_call(
        functools.partial(unpack_kernel, scale),
        out_shape=(shape((27, channels, channels), F32),) * 2,
        in_specs=[VM] * 2,
        out_specs=(VM,) * 2,
        compiler_params=params(),
        cost_estimate=cost(0, 10),
        name="unpack",
    )(own.reshape(packed.shape), other.reshape(packed.shape))
    return grad_volume, first_grad, second_grad


def solution(mesh):
    placed = (
        P(("groups", "gz"), None, None, None),
        P(("groups", "gz"), None, None, None),
        P(),
        P(),
    )
    return jax.shard_map(
        shards,
        mesh=mesh,
        in_specs=placed,
        out_specs=(
            P(("groups", "gz"), None, None, None),
            P("groups", None, None),
            P("groups", None, None),
        ),
        check_vma=False,
    )
```

```python
import functools
import math

import jax
import jax.numpy as jnp
from jax import lax
from jax.experimental import pallas as pl
from jax.experimental.pallas import tpu as pltpu
from jax.sharding import PartitionSpec as P

F32 = jnp.float32
BF16 = jnp.bfloat16
VM = pl.BlockSpec(memory_space=pltpu.VMEM)
ANY = pl.BlockSpec(memory_space=pl.ANY)
LIMIT = 24 << 20


def relayout(src, dst, wide):
    channels, rows, columns = src.shape
    wide[...] = src[...].astype(F32).reshape(channels * rows, columns)
    for row in range(rows):
        dst[:, (row + 1) * columns : (row + 2) * columns] = wide[
            pl.ds(row, channels, stride=rows), :
        ].astype(BF16)


def zero_rows(padded, columns):
    layers, channels, width = padded.shape
    zeros = jnp.zeros((channels, columns), BF16)
    for layer in range(layers):
        padded[layer, :, :columns] = zeros
        padded[layer, :, width - columns :] = zeros


def windows(three, columns, flat):
    return jnp.concatenate(
        [layer[:, b * columns : b * columns + flat] for layer in three for b in range(3)], axis=0
    )


def shifted(field, step, columns):
    channels, flat = field.shape
    lane = lax.broadcasted_iota(jnp.int32, (channels, columns), 1)
    keep = lane != (0 if step == 1 else columns - 1)
    return jnp.concatenate(
        [
            jnp.where(keep, pltpu.roll(field[:, at : at + columns], step % columns, 1), 0.0)
            for at in range(0, flat, columns)
        ],
        axis=1,
    )


def joined(three, step, columns):
    channels = three.shape[0] // 3
    return (
        three[channels : 2 * channels]
        + shifted(three[:channels], step, columns)
        + shifted(three[2 * channels :], -step, columns)
    )


def column_taps(field, step, columns):
    return jnp.concatenate(
        [
            shifted(field, -step, columns).astype(BF16),
            field.astype(BF16),
            shifted(field, step, columns).astype(BF16),
        ],
        axis=0,
    )


def one_layer(near_volume, near_cot, forward, adjoint, columns, flat):
    volume_windows = windows(near_volume, columns, flat)
    cot_windows = windows(near_cot, columns, flat)
    hidden = joined(jnp.dot(forward, volume_windows, preferred_element_type=F32), 1, columns)
    back_act = joined(jnp.dot(adjoint, cot_windows, preferred_element_type=F32), -1, columns)
    sigmoid_h = jax.nn.sigmoid(hidden)
    activation = (hidden * sigmoid_h).astype(BF16)
    grad_hidden = (back_act * sigmoid_h * (1.0 + hidden * (1.0 - sigmoid_h))).astype(BF16)
    last = (((1,), (1,)), ((), ()))
    first_term = lax.dot_general(
        volume_windows,
        column_taps(grad_hidden.astype(F32), 1, columns),
        last,
        preferred_element_type=F32,
    )
    second_term = lax.dot_general(
        column_taps(activation.astype(F32), -1, columns),
        cot_windows,
        last,
        preferred_element_type=F32,
    )
    return grad_hidden, first_term, second_term


def forward_taps(taps, out):
    for number in range(9):
        channels = taps.shape[1]
        row = jnp.concatenate([taps[3 * number + c].astype(F32) for c in range(3)], axis=1)
        out[:, number * channels : (number + 1) * channels] = row.T.astype(BF16)


def adjoint_taps(taps, out):
    channels = taps.shape[1]
    for c in range(3):
        out[c * channels : (c + 1) * channels, :] = jnp.concatenate(
            [taps[3 * (8 - number) + c] for number in range(9)], axis=1
        )


def inner_kernel(
    volume,
    cot,
    on_chip,
    first_k,
    second_k,
    volume_o,
    cot_o,
    grad_o,
    edge_o,
    first_o,
    second_o,
    forward,
    adjoint,
    flipped,
    wide,
):
    layers, channels, rows, columns = volume.shape
    flat = rows * columns
    forward_taps(first_k, forward)
    adjoint_taps(second_k, adjoint)
    adjoint_taps(first_k, flipped)
    zero_rows(volume_o, columns)
    zero_rows(cot_o, columns)
    core = lax.axis_index("gz") & 1
    rim = (layers + 1) * (1 - core)
    for layer in range(layers):
        relayout(volume.at[layer], volume_o.at[layer + 1], wide.at[0])
        relayout(cot.at[layer], cot_o.at[layer + 1], wide.at[1])
    relayout(on_chip.at[0, pl.ds(0, channels)], volume_o.at[rim], wide.at[0])
    relayout(on_chip.at[0, pl.ds(channels, channels)], cot_o.at[rim], wide.at[1])
    edge = 1 + (layers - 1) * (1 - core)
    for place, layer in enumerate([*range(2, layers), edge]):
        grad_hidden, first_term, second_term = one_layer(
            [volume_o[layer + a] for a in (-1, 0, 1)],
            [cot_o[layer + a] for a in (-1, 0, 1)],
            forward[...],
            adjoint[...],
            columns,
            flat,
        )
        if place < layers - 2:
            grad_o[place] = grad_hidden
        else:
            edge_o[0] = grad_hidden
        if place == 0:
            first_o[...] = first_term
            second_o[...] = second_term
        else:
            first_o[...] += first_term
            second_o[...] += second_term


def pack_first(term):
    half = term.shape[0] // 2
    return term[:, :128], jnp.concatenate([term[:half, 128:], term[half:, 128:]], axis=1)


def pack_second(term):
    half = term.shape[0] // 2
    pieces = [term[:, at : at + 128] for at in range(0, 512, 128)]
    return pieces + [jnp.concatenate([term[:half, 512:], term[half:, 512:]], axis=1)]


def put_rows(dst, pieces):
    at = 0
    for piece in pieces:
        dst[at : at + piece.shape[0], :] = piece
        at += piece.shape[0]


def outer_kernel(
    off_chip,
    volume_p,
    cot_p,
    first_in,
    second_in,
    forward,
    adjoint,
    edge_o,
    mine_o,
    theirs_o,
    near,
    wide,
):
    layers = volume_p.shape[0] - 2
    channels = off_chip.shape[1] // 2
    rows, columns = off_chip.shape[2:]
    flat = rows * columns
    core = lax.axis_index("gz") & 1
    edge = 1 + (layers - 1) * core
    for kind, padded in enumerate((volume_p, cot_p)):
        rim = near.at[kind, 2 * core]
        zeros = jnp.zeros((channels, columns), BF16)
        rim[:, :columns] = zeros
        rim[:, columns + flat :] = zeros
        relayout(off_chip.at[0, pl.ds(kind * channels, channels)], rim, wide.at[kind])
        near[kind, 1] = padded[edge]
        near[kind, 2 - 2 * core] = padded[edge + 1 - 2 * core]
    grad_hidden, first_term, second_term = one_layer(
        [near[0, a] for a in range(3)],
        [near[1, a] for a in range(3)],
        forward[...],
        adjoint[...],
        columns,
        flat,
    )
    edge_o[0] = grad_hidden
    first = pack_first(first_in[...] + first_term)
    second = pack_second(second_in[...] + second_term)

    @pl.when(core == 0)
    def _():
        put_rows(mine_o, first)
        put_rows(theirs_o, second)

    @pl.when(core == 1)
    def _():
        put_rows(mine_o, second)
        put_rows(theirs_o, first)


def volume_kernel(
    on_chip, off_chip, inner, on_edge, off_edge, cot, adjoint, out, padded, wide, buf, out_sem
):
    layers, channels, rows, columns = cot.shape
    flat = rows * columns
    core = lax.axis_index("gz") & 1
    zero_rows(padded, columns)
    middle = slice(columns, columns + flat)
    padded[(1 - core) * (layers + 1), :, middle] = on_chip[0]
    padded[core * (layers + 1), :, middle] = off_chip[0]
    padded[1 + (layers - 1) * (1 - core), :, middle] = on_edge[0]
    padded[1 + (layers - 1) * core, :, middle] = off_edge[0]
    for layer in range(layers - 2):
        padded[layer + 2, :, middle] = inner[layer]
    for layer in range(layers):
        three = jnp.dot(
            adjoint[...],
            windows([padded[layer + a] for a in range(3)], columns, flat),
            preferred_element_type=F32,
        )
        summed = joined(three, -1, columns)
        scratch = wide.at[layer % 2]
        for row in range(rows):
            scratch[pl.ds(row, channels, stride=rows), :] = summed[
                :, row * columns : (row + 1) * columns
            ]
        buf[layer] = (
            cot[layer].astype(F32) + scratch[...].reshape(channels, rows, columns)
        ).astype(BF16)
        pltpu.make_async_copy(buf.at[layer], out.at[layer], out_sem.at[layer]).start()
    for layer in range(layers):
        pltpu.make_async_copy(buf.at[layer], out.at[layer], out_sem.at[layer]).wait()


def unpack_kernel(scale, mine, other, first_o, second_o):
    channels = first_o.shape[1]

    def unpack_first(src):
        half = 9 * channels // 2
        for number in range(9):
            at = number * channels
            for c in range(2):
                first_o[3 * number + c] = (
                    src[at : at + channels, c * channels : (c + 1) * channels].astype(F32) * scale
                )
            for low in range(0, channels, channels // 2):
                row = at + low
                part, side = (row, 0) if row < half else (row - half, 1)
                first_o[3 * number + 2, low : low + channels // 2] = (
                    src[
                        9 * channels + part : 9 * channels + part + channels // 2,
                        side * channels : (side + 1) * channels,
                    ].astype(F32)
                    * scale
                )

    def unpack_second(src):
        half = 3 * channels // 2
        for number in range(9):
            for c in range(3):
                tap = 3 * (8 - number) + c
                if number < 8:
                    at = (number // 2) * 3 * channels + c * channels
                    side = number % 2
                    second_o[tap] = (
                        src[at : at + channels, side * channels : (side + 1) * channels].astype(F32)
                        * scale
                    )
                    continue
                for low in range(0, channels, channels // 2):
                    row = c * channels + low
                    part, side = (row, 0) if row < half else (row - half, 1)
                    second_o[tap, low : low + channels // 2] = (
                        src[
                            12 * channels + part : 12 * channels + part + channels // 2,
                            side * channels : (side + 1) * channels,
                        ].astype(F32)
                        * scale
                    )

    core = lax.axis_index("gz") & 1

    @pl.when(core == 0)
    def _():
        unpack_first(mine)
        unpack_second(other)

    @pl.when(core == 1)
    def _():
        unpack_first(other)
        unpack_second(mine)


def swapped(array, mask):
    return lax.ppermute(array, "gz", [(i, i ^ mask) for i in range(lax.axis_size("gz"))])


def swapped_chips(array):
    pairs = [(i, i + 1) for i in range(1, lax.axis_size("gz") - 1, 2)]
    return lax.ppermute(array, "gz", pairs + [(j, i) for i, j in pairs])


def picked(stack, i):
    return lax.dynamic_index_in_dim(stack, i, 0, keepdims=False)


def quarter_of(mine, theirs):
    quarter = (lax.axis_index("gz") >> 1) & 3
    stack = (mine + swapped(theirs, 1)).reshape(4, -1, *mine.shape[1:])
    sent = [picked(stack, quarter ^ other) for other in (1, 2, 3)]
    return picked(stack, quarter), sent


def whole_of(total):
    mask = 16
    while mask < lax.axis_size("gz"):
        total = total + swapped(total, mask)
        mask *= 2
    return total.astype(BF16)


def in_order(found, shape):
    quarter = (lax.axis_index("gz") >> 1) & 3
    stack = jnp.stack(found)
    return jnp.stack([picked(stack, quarter ^ place) for place in range(4)]).reshape(shape)


def shards(volume, cotangent, first_kernel, second_kernel):
    layers, channels, rows, columns = volume.shape
    flat = rows * columns
    wide = flat + 2 * columns
    devices = lax.axis_size("gz")
    core = lax.axis_index("gz") & 1
    edge = jnp.where(core == 0, layers - 1, 0)
    other_edge = layers - 1 - edge
    near = [jnp.concatenate([lax.dynamic_slice_in_dim(x, at, 1) for x in (volume, cotangent)], axis=1) for at in (edge, other_edge)]
    on_chip, off_chip = swapped(near[0], 1), swapped_chips(near[1])

    conv_flops = 2 * 27 * channels * channels * flat
    layer_bytes = 2 * channels * flat

    def cost(passes, moved):
        return pl.CostEstimate(
            flops=passes * conv_flops, bytes_accessed=moved * layer_bytes, transcendentals=0
        )

    def params():
        return pltpu.CompilerParams(vmem_limit_bytes=LIMIT)

    shape = jax.ShapeDtypeStruct
    taps = shape((3 * channels, 9 * channels), BF16)
    layer = shape((1, channels, flat), BF16)
    volume_p, cot_p, inner, on_edge, first_in, second_in, forward, adjoint, flipped = pl.pallas_call(
        inner_kernel,
        out_shape=(
            shape((layers + 2, channels, wide), BF16),
            shape((layers + 2, channels, wide), BF16),
            shape((layers - 2, channels, flat), BF16),
            layer,
            shape((9 * channels, 3 * channels), F32),
            shape((3 * channels, 9 * channels), F32),
            taps,
            taps,
            taps,
        ),
        in_specs=[VM] * 5,
        out_specs=(VM,) * 9,
        scratch_shapes=[pltpu.VMEM((2, channels * rows, columns), F32)],
        compiler_params=params(),
        cost_estimate=cost(4 * (layers - 1), 4 * layers),
        name="inner",
    )(volume, cotangent, on_chip, first_kernel, second_kernel)

    packed = shape((27 * channels * channels // 128, 128), F32)
    off_edge, mine, theirs = pl.pallas_call(
        outer_kernel,
        out_shape=(layer, packed, packed),
        in_specs=[VM] * 7,
        out_specs=(VM,) * 3,
        scratch_shapes=[
            pltpu.VMEM((2, 3, channels, wide), BF16),
            pltpu.VMEM((2, channels * rows, columns), F32),
        ],
        compiler_params=params(),
        cost_estimate=cost(4, 8),
        name="outer",
    )(off_chip, volume_p, cot_p, first_in, second_in, forward, adjoint)

    tiles = (packed.shape[0] // 8, 8, 128)
    own, sent = quarter_of(mine.reshape(tiles), theirs.reshape(tiles))
    sent, on_edge = lax.optimization_barrier((sent, on_edge))
    total = sum(swapped(sent[other - 1], 2 * other) for other in (1, 2, 3)) + own
    on_chip_g = swapped(on_edge, 1)
    total, off_edge = lax.optimization_barrier((total.astype(BF16), off_edge))
    off_chip_g = swapped_chips(off_edge)
    further = swapped(total, 8)
    total = total.astype(F32) + further.astype(F32)
    total, flipped = lax.optimization_barrier((whole_of(total), flipped))
    grad_volume = pl.pallas_call(
        volume_kernel,
        out_shape=shape(volume.shape, BF16),
        in_specs=[VM] * 7,
        out_specs=ANY,
        scratch_shapes=[
            pltpu.VMEM((layers + 2, channels, wide), BF16),
            pltpu.VMEM((2, channels * rows, columns), F32),
            pltpu.VMEM(volume.shape, BF16),
            pltpu.SemaphoreType.DMA((layers,)),
        ],
        compiler_params=params(),
        cost_estimate=cost(layers, 4 * layers),
        name="volume",
    )(on_chip_g, off_chip_g, inner, on_edge, off_edge, cotangent, flipped)

    found = [total] + [swapped(total, 2 * other) for other in (1, 2, 3)]
    found, grad_volume = lax.optimization_barrier((found, grad_volume))
    own = in_order(found, tiles)
    other = swapped(own, 1)
    scale = 1.0 / math.sqrt(layers * devices * flat)
    first_grad, second_grad = pl.pallas_call(
        functools.partial(unpack_kernel, scale),
        out_shape=(shape((27, channels, channels), F32),) * 2,
        in_specs=[VM] * 2,
        out_specs=(VM,) * 2,
        compiler_params=params(),
        cost_estimate=cost(0, 10),
        name="unpack",
    )(own.reshape(packed.shape), other.reshape(packed.shape))
    return grad_volume, first_grad, second_grad


def solution(mesh):
    placed = (
        P(("groups", "gz"), None, None, None),
        P(("groups", "gz"), None, None, None),
        P(),
        P(),
    )
    return jax.shard_map(
        shards,
        mesh=mesh,
        in_specs=placed,
        out_specs=(
            P(("groups", "gz"), None, None, None),
            P("groups", None, None),
            P("groups", None, None),
        ),
        check_vma=False,
    )
```

```python
import functools
import math

import jax
import jax.numpy as jnp
from jax import lax
from jax.experimental import pallas as pl
from jax.experimental.pallas import tpu as pltpu
from jax.sharding import PartitionSpec as P

F32 = jnp.float32
BF16 = jnp.bfloat16
VM = pl.BlockSpec(memory_space=pltpu.VMEM)
ANY = pl.BlockSpec(memory_space=pl.ANY)
LIMIT = 24 << 20


def relayout(src, dst, wide):
    channels, rows, columns = src.shape
    wide[...] = src[...].astype(F32).reshape(channels * rows, columns)
    for row in range(rows):
        dst[:, (row + 1) * columns : (row + 2) * columns] = wide[
            pl.ds(row, channels, stride=rows), :
        ].astype(BF16)


def zero_rows(padded, columns):
    layers, channels, width = padded.shape
    zeros = jnp.zeros((channels, columns), BF16)
    for layer in range(layers):
        padded[layer, :, :columns] = zeros
        padded[layer, :, width - columns :] = zeros


def windows(three, columns, flat):
    return jnp.concatenate(
        [layer[:, b * columns : b * columns + flat] for layer in three for b in range(3)], axis=0
    )


def shifted(field, step, columns):
    channels, flat = field.shape
    lane = lax.broadcasted_iota(jnp.int32, (channels, columns), 1)
    keep = lane != (0 if step == 1 else columns - 1)
    return jnp.concatenate(
        [
            jnp.where(keep, pltpu.roll(field[:, at : at + columns], step % columns, 1), 0.0)
            for at in range(0, flat, columns)
        ],
        axis=1,
    )


def joined(three, step, columns):
    channels = three.shape[0] // 3
    return (
        three[channels : 2 * channels]
        + shifted(three[:channels], step, columns)
        + shifted(three[2 * channels :], -step, columns)
    )


def column_taps(field, step, columns):
    return jnp.concatenate(
        [
            shifted(field, -step, columns).astype(BF16),
            field.astype(BF16),
            shifted(field, step, columns).astype(BF16),
        ],
        axis=0,
    )


def one_layer(near_volume, near_cot, forward, adjoint, columns, flat):
    volume_windows = windows(near_volume, columns, flat)
    cot_windows = windows(near_cot, columns, flat)
    hidden = joined(jnp.dot(forward, volume_windows, preferred_element_type=F32), 1, columns)
    back_act = joined(jnp.dot(adjoint, cot_windows, preferred_element_type=F32), -1, columns)
    sigmoid_h = jax.nn.sigmoid(hidden)
    activation = (hidden * sigmoid_h).astype(BF16)
    grad_hidden = (back_act * sigmoid_h * (1.0 + hidden * (1.0 - sigmoid_h))).astype(BF16)
    last = (((1,), (1,)), ((), ()))
    first_term = lax.dot_general(
        volume_windows,
        column_taps(grad_hidden.astype(F32), 1, columns),
        last,
        preferred_element_type=F32,
    )
    second_term = lax.dot_general(
        column_taps(activation.astype(F32), -1, columns),
        cot_windows,
        last,
        preferred_element_type=F32,
    )
    return grad_hidden, first_term, second_term


def forward_taps(taps, out):
    for number in range(9):
        channels = taps.shape[1]
        row = jnp.concatenate([taps[3 * number + c].astype(F32) for c in range(3)], axis=1)
        out[:, number * channels : (number + 1) * channels] = row.T.astype(BF16)


def adjoint_taps(taps, out):
    channels = taps.shape[1]
    for c in range(3):
        out[c * channels : (c + 1) * channels, :] = jnp.concatenate(
            [taps[3 * (8 - number) + c] for number in range(9)], axis=1
        )


def edges_kernel(volume, cot, near_o, far_o, sems):
    layers, channels = volume.shape[:2]
    core = lax.axis_index("gz") & 1
    edge = (layers - 1) * (1 - core)
    copies = []
    for out, at in ((far_o, layers - 1 - edge), (near_o, edge)):
        for kind, src in enumerate((volume, cot)):
            copies.append(
                pltpu.make_async_copy(
                    src.at[at], out.at[0, pl.ds(kind * channels, channels)], sems.at[len(copies)]
                )
            )
            copies[-1].start()
    for copy in copies:
        copy.wait()


def inner_kernel(
    volume,
    cot,
    on_chip,
    first_k,
    second_k,
    volume_o,
    cot_o,
    grad_o,
    edge_o,
    first_o,
    second_o,
    forward,
    adjoint,
    flipped,
    wide,
):
    layers, channels, rows, columns = volume.shape
    flat = rows * columns
    forward_taps(first_k, forward)
    adjoint_taps(second_k, adjoint)
    adjoint_taps(first_k, flipped)
    zero_rows(volume_o, columns)
    zero_rows(cot_o, columns)
    core = lax.axis_index("gz") & 1
    rim = (layers + 1) * (1 - core)
    for layer in range(layers):
        relayout(volume.at[layer], volume_o.at[layer + 1], wide.at[0])
        relayout(cot.at[layer], cot_o.at[layer + 1], wide.at[1])
    relayout(on_chip.at[0, pl.ds(0, channels)], volume_o.at[rim], wide.at[0])
    relayout(on_chip.at[0, pl.ds(channels, channels)], cot_o.at[rim], wide.at[1])
    edge = 1 + (layers - 1) * (1 - core)
    for place, layer in enumerate([*range(2, layers), edge]):
        grad_hidden, first_term, second_term = one_layer(
            [volume_o[layer + a] for a in (-1, 0, 1)],
            [cot_o[layer + a] for a in (-1, 0, 1)],
            forward[...],
            adjoint[...],
            columns,
            flat,
        )
        if place < layers - 2:
            grad_o[place] = grad_hidden
        else:
            edge_o[0] = grad_hidden
        if place == 0:
            first_o[...] = first_term
            second_o[...] = second_term
        else:
            first_o[...] += first_term
            second_o[...] += second_term


def pack_first(term):
    half = term.shape[0] // 2
    return term[:, :128], jnp.concatenate([term[:half, 128:], term[half:, 128:]], axis=1)


def pack_second(term):
    half = term.shape[0] // 2
    pieces = [term[:, at : at + 128] for at in range(0, 512, 128)]
    return pieces + [jnp.concatenate([term[:half, 512:], term[half:, 512:]], axis=1)]


def put_rows(dst, pieces):
    at = 0
    for piece in pieces:
        dst[at : at + piece.shape[0], :] = piece
        at += piece.shape[0]


def outer_kernel(
    off_chip,
    volume_p,
    cot_p,
    first_in,
    second_in,
    forward,
    adjoint,
    edge_o,
    mine_o,
    theirs_o,
    near,
    wide,
):
    layers = volume_p.shape[0] - 2
    channels = off_chip.shape[1] // 2
    rows, columns = off_chip.shape[2:]
    flat = rows * columns
    core = lax.axis_index("gz") & 1
    edge = 1 + (layers - 1) * core
    for kind, padded in enumerate((volume_p, cot_p)):
        rim = near.at[kind, 2 * core]
        zeros = jnp.zeros((channels, columns), BF16)
        rim[:, :columns] = zeros
        rim[:, columns + flat :] = zeros
        relayout(off_chip.at[0, pl.ds(kind * channels, channels)], rim, wide.at[kind])
        near[kind, 1] = padded[edge]
        near[kind, 2 - 2 * core] = padded[edge + 1 - 2 * core]
    grad_hidden, first_term, second_term = one_layer(
        [near[0, a] for a in range(3)],
        [near[1, a] for a in range(3)],
        forward[...],
        adjoint[...],
        columns,
        flat,
    )
    edge_o[0] = grad_hidden
    first = pack_first(first_in[...] + first_term)
    second = pack_second(second_in[...] + second_term)

    @pl.when(core == 0)
    def _():
        put_rows(mine_o, first)
        put_rows(theirs_o, second)

    @pl.when(core == 1)
    def _():
        put_rows(mine_o, second)
        put_rows(theirs_o, first)


def volume_kernel(
    on_chip, off_chip, inner, on_edge, off_edge, cot, adjoint, out, padded, wide, buf, out_sem
):
    layers, channels, rows, columns = cot.shape
    flat = rows * columns
    core = lax.axis_index("gz") & 1
    zero_rows(padded, columns)
    middle = slice(columns, columns + flat)
    padded[(1 - core) * (layers + 1), :, middle] = on_chip[0]
    padded[core * (layers + 1), :, middle] = off_chip[0]
    padded[1 + (layers - 1) * (1 - core), :, middle] = on_edge[0]
    padded[1 + (layers - 1) * core, :, middle] = off_edge[0]
    for layer in range(layers - 2):
        padded[layer + 2, :, middle] = inner[layer]
    for layer in range(layers):
        three = jnp.dot(
            adjoint[...],
            windows([padded[layer + a] for a in range(3)], columns, flat),
            preferred_element_type=F32,
        )
        summed = joined(three, -1, columns)
        scratch = wide.at[layer % 2]
        for row in range(rows):
            scratch[pl.ds(row, channels, stride=rows), :] = summed[
                :, row * columns : (row + 1) * columns
            ]
        buf[layer] = (
            cot[layer].astype(F32) + scratch[...].reshape(channels, rows, columns)
        ).astype(BF16)
        pltpu.make_async_copy(buf.at[layer], out.at[layer], out_sem.at[layer]).start()
    for layer in range(layers):
        pltpu.make_async_copy(buf.at[layer], out.at[layer], out_sem.at[layer]).wait()


def unpack_first(src, dst, number, scale):
    channels = dst.shape[1]
    half = 9 * channels // 2
    at = number * channels
    for c in range(2):
        dst[3 * number + c] = (
            src[at : at + channels, c * channels : (c + 1) * channels].astype(F32) * scale
        )
    for low in range(0, channels, channels // 2):
        row = at + low
        part, side = (row, 0) if row < half else (row - half, 1)
        part += 9 * channels
        dst[3 * number + 2, low : low + channels // 2] = (
            src[part : part + channels // 2, side * channels : (side + 1) * channels].astype(F32)
            * scale
        )


def unpack_second(src, dst, number, scale):
    channels = dst.shape[1]
    half = 3 * channels // 2
    place = 8 - number
    for c in range(3):
        if place < 8:
            at = (place // 2) * 3 * channels + c * channels
            side = place % 2
            dst[3 * number + c] = (
                src[at : at + channels, side * channels : (side + 1) * channels].astype(F32)
                * scale
            )
            continue
        for low in range(0, channels, channels // 2):
            row = c * channels + low
            part, side = (row, 0) if row < half else (row - half, 1)
            part += 12 * channels
            dst[3 * number + c, low : low + channels // 2] = (
                src[part : part + channels // 2, side * channels : (side + 1) * channels].astype(
                    F32
                )
                * scale
            )


def unpack_kernel(scale, swap, src, *refs):
    first_o, second_o, buf, sems = refs[-4:]
    core = lax.axis_index("gz") & 1

    def run(unpack, out):
        copies = []
        for depth in range(3):
            for number in range(3 * depth, 3 * depth + 3):
                unpack(src, buf, number, scale)
            part = pl.ds(9 * depth, 9)
            copies.append(pltpu.make_async_copy(buf.at[part], out.at[part], sems.at[depth]))
            copies[-1].start()
        for copy in copies:
            copy.wait()

    @pl.when(core == swap)
    def _():
        run(unpack_first, first_o)

    @pl.when(core == 1 - swap)
    def _():
        run(unpack_second, second_o)


def swapped(array, mask):
    return lax.ppermute(array, "gz", [(i, i ^ mask) for i in range(lax.axis_size("gz"))])


def swapped_chips(array):
    pairs = [(i, i + 1) for i in range(1, lax.axis_size("gz") - 1, 2)]
    return lax.ppermute(array, "gz", pairs + [(j, i) for i, j in pairs])


def picked(stack, i):
    return lax.dynamic_index_in_dim(stack, i, 0, keepdims=False)


def quarter_of(mine, theirs):
    quarter = (lax.axis_index("gz") >> 1) & 3
    stack = (mine + swapped(theirs, 1)).reshape(4, -1, *mine.shape[1:])
    sent = [picked(stack, quarter ^ other).astype(BF16) for other in (1, 2, 3)]
    return picked(stack, quarter), sent


def whole_of(total):
    mask = 16
    while mask < lax.axis_size("gz"):
        total = total + swapped(total, mask)
        mask *= 2
    return total.astype(BF16)


def in_order(found, shape):
    quarter = (lax.axis_index("gz") >> 1) & 3
    stack = jnp.stack(found)
    return jnp.stack([picked(stack, quarter ^ place) for place in range(4)]).reshape(shape)


def shards(volume, cotangent, first_kernel, second_kernel):
    layers, channels, rows, columns = volume.shape
    flat = rows * columns
    wide = flat + 2 * columns
    devices = lax.axis_size("gz")
    conv_flops = 2 * 27 * channels * channels * flat
    layer_bytes = 2 * channels * flat

    def cost(passes, moved):
        return pl.CostEstimate(
            flops=passes * conv_flops, bytes_accessed=moved * layer_bytes, transcendentals=0
        )

    def params():
        return pltpu.CompilerParams(vmem_limit_bytes=LIMIT)

    shape = jax.ShapeDtypeStruct
    near, far = pl.pallas_call(
        edges_kernel,
        out_shape=(shape((1, 2 * channels, rows, columns), BF16),) * 2,
        in_specs=[pl.BlockSpec(memory_space=pltpu.HBM)] * 2,
        out_specs=(VM,) * 2,
        scratch_shapes=[pltpu.SemaphoreType.DMA((4,))],
        compiler_params=params(),
        cost_estimate=cost(0, 8),
        name="edges",
    )(volume, cotangent)
    off_chip = swapped_chips(far)
    on_chip = swapped(near, 1)

    taps = shape((3 * channels, 9 * channels), BF16)
    layer = shape((1, channels, flat), BF16)
    volume_p, cot_p, inner, on_edge, first_in, second_in, forward, adjoint, flipped = pl.pallas_call(
        inner_kernel,
        out_shape=(
            shape((layers + 2, channels, wide), BF16),
            shape((layers + 2, channels, wide), BF16),
            shape((layers - 2, channels, flat), BF16),
            layer,
            shape((9 * channels, 3 * channels), F32),
            shape((3 * channels, 9 * channels), F32),
            taps,
            taps,
            taps,
        ),
        in_specs=[VM] * 5,
        out_specs=(VM,) * 9,
        scratch_shapes=[pltpu.VMEM((2, channels * rows, columns), F32)],
        compiler_params=params(),
        cost_estimate=cost(4 * (layers - 1), 4 * layers),
        name="inner",
    )(volume, cotangent, on_chip, first_kernel, second_kernel)

    packed = shape((27 * channels * channels // 128, 128), F32)
    off_edge, mine, theirs = pl.pallas_call(
        outer_kernel,
        out_shape=(layer, packed, packed),
        in_specs=[VM] * 7,
        out_specs=(VM,) * 3,
        scratch_shapes=[
            pltpu.VMEM((2, 3, channels, wide), BF16),
            pltpu.VMEM((2, channels * rows, columns), F32),
        ],
        compiler_params=params(),
        cost_estimate=cost(4, 8),
        name="outer",
    )(off_chip, volume_p, cot_p, first_in, second_in, forward, adjoint)

    tiles = (packed.shape[0] // 8, 8, 128)
    own, sent = quarter_of(mine.reshape(tiles), theirs.reshape(tiles))
    sent, on_edge = lax.optimization_barrier((sent, on_edge))
    total = own
    for other in (1, 2, 3):
        total = total + swapped(sent[other - 1], 2 * other).astype(F32)
    on_chip_g = swapped(on_edge, 1)
    total, off_edge = lax.optimization_barrier((total, off_edge))
    off_chip_g = swapped_chips(off_edge)
    total = total + swapped(total, 8)
    total, flipped = lax.optimization_barrier((whole_of(total), flipped))
    grad_volume = pl.pallas_call(
        volume_kernel,
        out_shape=shape(volume.shape, BF16),
        in_specs=[VM] * 7,
        out_specs=ANY,
        scratch_shapes=[
            pltpu.VMEM((layers + 2, channels, wide), BF16),
            pltpu.VMEM((2, channels * rows, columns), F32),
            pltpu.VMEM(volume.shape, BF16),
            pltpu.SemaphoreType.DMA((layers,)),
        ],
        compiler_params=params(),
        cost_estimate=cost(layers, 4 * layers),
        name="volume",
    )(on_chip_g, off_chip_g, inner, on_edge, off_edge, cotangent, flipped)

    found = [total] + [swapped(total, 2 * other) for other in (1, 2, 3)]
    found, grad_volume = lax.optimization_barrier((found, grad_volume))
    own = in_order(found, tiles)
    other = swapped(own, 1)
    scale = 1.0 / math.sqrt(layers * devices * flat)
    grads = ()
    for swap, part in enumerate((own, other)):
        grads = pl.pallas_call(
            functools.partial(unpack_kernel, scale, swap),
            out_shape=(shape((27, channels, channels), F32),) * 2,
            in_specs=[VM] + [ANY] * len(grads),
            out_specs=(ANY,) * 2,
            scratch_shapes=[
                pltpu.VMEM((27, channels, channels), F32),
                pltpu.SemaphoreType.DMA((3,)),
            ],
            input_output_aliases={1: 0, 2: 1} if grads else {},
            compiler_params=params(),
            cost_estimate=cost(0, 6),
            name="unpack",
        )(part.reshape(packed.shape), *grads)
    first_grad, second_grad = grads
    return grad_volume, first_grad, second_grad


def solution(mesh):
    placed = (
        P(("groups", "gz"), None, None, None),
        P(("groups", "gz"), None, None, None),
        P(),
        P(),
    )
    return jax.shard_map(
        shards,
        mesh=mesh,
        in_specs=placed,
        out_specs=(
            P(("groups", "gz"), None, None, None),
            P("groups", None, None),
            P("groups", None, None),
        ),
        check_vma=False,
    )
```

```python
import functools
import math

import jax
import jax.numpy as jnp
from jax import lax
from jax.experimental import pallas as pl
from jax.experimental.pallas import tpu as pltpu
from jax.sharding import PartitionSpec as P

F32 = jnp.float32
BF16 = jnp.bfloat16
VM = pl.BlockSpec(memory_space=pltpu.VMEM)
ANY = pl.BlockSpec(memory_space=pl.ANY)
LIMIT = 24 << 20


def relayout(src, dst, wide):
    channels, rows, columns = src.shape
    wide[...] = src[...].astype(F32).reshape(channels * rows, columns)
    for row in range(rows):
        dst[:, (row + 1) * columns : (row + 2) * columns] = wide[
            pl.ds(row, channels, stride=rows), :
        ].astype(BF16)


def zero_rows(padded, columns):
    layers, channels, width = padded.shape
    zeros = jnp.zeros((channels, columns), BF16)
    for layer in range(layers):
        padded[layer, :, :columns] = zeros
        padded[layer, :, width - columns :] = zeros


def windows(three, columns, flat):
    return jnp.concatenate(
        [layer[:, b * columns : b * columns + flat] for layer in three for b in range(3)], axis=0
    )


def shifted(field, step, columns):
    channels, flat = field.shape
    lane = lax.broadcasted_iota(jnp.int32, (channels, columns), 1)
    keep = lane != (0 if step == 1 else columns - 1)
    return jnp.concatenate(
        [
            jnp.where(keep, pltpu.roll(field[:, at : at + columns], step % columns, 1), 0.0)
            for at in range(0, flat, columns)
        ],
        axis=1,
    )


def joined(three, step, columns):
    channels = three.shape[0] // 3
    return (
        three[channels : 2 * channels]
        + shifted(three[:channels], step, columns)
        + shifted(three[2 * channels :], -step, columns)
    )


def column_taps(field, step, columns):
    return jnp.concatenate(
        [
            shifted(field, -step, columns).astype(BF16),
            field.astype(BF16),
            shifted(field, step, columns).astype(BF16),
        ],
        axis=0,
    )


def one_layer(near_volume, near_cot, products, columns, flat):
    volume_windows = windows(near_volume, columns, flat)
    cot_windows = windows(near_cot, columns, flat)
    of_volume, of_cot = products(volume_windows, cot_windows)
    hidden = joined(of_volume, 1, columns)
    back_act = joined(of_cot, -1, columns)
    sigmoid_h = jax.nn.sigmoid(hidden)
    activation = (hidden * sigmoid_h).astype(BF16)
    grad_hidden = (back_act * sigmoid_h * (1.0 + hidden * (1.0 - sigmoid_h))).astype(BF16)
    last = (((1,), (1,)), ((), ()))
    first_term = lax.dot_general(
        volume_windows,
        column_taps(grad_hidden.astype(F32), 1, columns),
        last,
        preferred_element_type=F32,
    )
    second_term = lax.dot_general(
        column_taps(activation.astype(F32), -1, columns),
        cot_windows,
        last,
        preferred_element_type=F32,
    )
    return grad_hidden, first_term, second_term


def forward_taps(taps, out):
    for number in range(9):
        channels = taps.shape[1]
        row = jnp.concatenate([taps[3 * number + c].astype(F32) for c in range(3)], axis=1)
        out[:, number * channels : (number + 1) * channels] = row.T.astype(BF16)


def adjoint_taps(taps, out):
    channels = taps.shape[1]
    for c in range(3):
        out[c * channels : (c + 1) * channels, :] = jnp.concatenate(
            [taps[3 * (8 - number) + c] for number in range(9)], axis=1
        )


def inner_kernel(
    volume,
    cot,
    on_chip,
    first_k,
    second_k,
    volume_o,
    cot_o,
    grad_o,
    edge_o,
    first_o,
    second_o,
    part_o,
    forward,
    adjoint,
    flipped,
    wide,
):
    layers, channels, rows, columns = volume.shape
    flat = rows * columns
    forward_taps(first_k, forward)
    adjoint_taps(second_k, adjoint)
    adjoint_taps(first_k, flipped)
    zero_rows(volume_o, columns)
    zero_rows(cot_o, columns)
    core = lax.axis_index("gz") & 1
    rim = (layers + 1) * (1 - core)
    for layer in range(layers):
        relayout(volume.at[layer], volume_o.at[layer + 1], wide.at[0])
        relayout(cot.at[layer], cot_o.at[layer + 1], wide.at[1])
    relayout(on_chip.at[0, pl.ds(0, channels)], volume_o.at[rim], wide.at[0])
    relayout(on_chip.at[0, pl.ds(channels, channels)], cot_o.at[rim], wide.at[1])
    edge = 1 + (layers - 1) * (1 - core)

    def products(volume_windows, cot_windows):
        return (
            jnp.dot(forward[...], volume_windows, preferred_element_type=F32),
            jnp.dot(adjoint[...], cot_windows, preferred_element_type=F32),
        )

    for place, layer in enumerate([*range(2, layers), edge]):
        grad_hidden, first_term, second_term = one_layer(
            [volume_o[layer + a] for a in (-1, 0, 1)],
            [cot_o[layer + a] for a in (-1, 0, 1)],
            products,
            columns,
            flat,
        )
        if place < layers - 2:
            grad_o[place] = grad_hidden
        else:
            edge_o[0] = grad_hidden
        if place == 0:
            first_o[...] = first_term
            second_o[...] = second_term
        else:
            first_o[...] += first_term
            second_o[...] += second_term

    layer = 1 + (layers - 1) * core
    for padded in (volume_o, cot_o):
        padded[(layers + 1) * core] = jnp.zeros(padded.shape[1:], BF16)
    part_o[0], part_o[1] = products(
        windows([volume_o[layer + a] for a in (-1, 0, 1)], columns, flat),
        windows([cot_o[layer + a] for a in (-1, 0, 1)], columns, flat),
    )


def pack_first(term):
    half = term.shape[0] // 2
    return term[:, :128], jnp.concatenate([term[:half, 128:], term[half:, 128:]], axis=1)


def pack_second(term):
    half = term.shape[0] // 2
    pieces = [term[:, at : at + 128] for at in range(0, 512, 128)]
    return pieces + [jnp.concatenate([term[:half, 512:], term[half:, 512:]], axis=1)]


def put_rows(dst, pieces):
    at = 0
    for piece in pieces:
        dst[at : at + piece.shape[0], :] = piece
        at += piece.shape[0]


def outer_kernel(
    off_chip,
    volume_p,
    cot_p,
    first_in,
    second_in,
    part,
    forward,
    adjoint,
    edge_o,
    mine_o,
    theirs_o,
    near,
    wide,
):
    layers = volume_p.shape[0] - 2
    channels = off_chip.shape[1] // 2
    rows, columns = off_chip.shape[2:]
    flat = rows * columns
    core = lax.axis_index("gz") & 1
    edge = 1 + (layers - 1) * core
    for kind, padded in enumerate((volume_p, cot_p)):
        rim = near.at[kind, 2 * core]
        zeros = jnp.zeros((channels, columns), BF16)
        rim[:, :columns] = zeros
        rim[:, columns + flat :] = zeros
        relayout(off_chip.at[0, pl.ds(kind * channels, channels)], rim, wide.at[kind])
        near[kind, 1] = padded[edge]
        near[kind, 2 - 2 * core] = padded[edge + 1 - 2 * core]
    depth = 3 * channels
    beyond = pl.ds(pl.multiple_of(2 * depth * core, 128), depth)

    def products(*unused):
        return [
            part[kind]
            + jnp.dot(
                taps[:, beyond],
                jnp.concatenate(
                    [near[kind, 2 * core, :, pl.ds(b * columns, flat)] for b in range(3)], axis=0
                ),
                preferred_element_type=F32,
            )
            for kind, taps in enumerate((forward, adjoint))
        ]

    grad_hidden, first_term, second_term = one_layer(
        [near[0, a] for a in range(3)],
        [near[1, a] for a in range(3)],
        products,
        columns,
        flat,
    )
    edge_o[0] = grad_hidden
    first = pack_first(first_in[...] + first_term)
    second = pack_second(second_in[...] + second_term)

    @pl.when(core == 0)
    def _():
        put_rows(mine_o, first)
        put_rows(theirs_o, second)

    @pl.when(core == 1)
    def _():
        put_rows(mine_o, second)
        put_rows(theirs_o, first)


def volume_kernel(
    on_chip, off_chip, inner, on_edge, off_edge, cot, adjoint, out, padded, wide, buf, out_sem
):
    layers, channels, rows, columns = cot.shape
    flat = rows * columns
    core = lax.axis_index("gz") & 1
    zero_rows(padded, columns)
    middle = slice(columns, columns + flat)
    padded[(1 - core) * (layers + 1), :, middle] = on_chip[0]
    padded[core * (layers + 1), :, middle] = off_chip[0]
    padded[1 + (layers - 1) * (1 - core), :, middle] = on_edge[0]
    padded[1 + (layers - 1) * core, :, middle] = off_edge[0]
    for layer in range(layers - 2):
        padded[layer + 2, :, middle] = inner[layer]
    for layer in range(layers):
        three = jnp.dot(
            adjoint[...],
            windows([padded[layer + a] for a in range(3)], columns, flat),
            preferred_element_type=F32,
        )
        summed = joined(three, -1, columns)
        scratch = wide.at[layer % 2]
        for row in range(rows):
            scratch[pl.ds(row, channels, stride=rows), :] = summed[
                :, row * columns : (row + 1) * columns
            ]
        buf[layer] = (
            cot[layer].astype(F32) + scratch[...].reshape(channels, rows, columns)
        ).astype(BF16)
        pltpu.make_async_copy(buf.at[layer], out.at[layer], out_sem.at[layer]).start()
    for layer in range(layers):
        pltpu.make_async_copy(buf.at[layer], out.at[layer], out_sem.at[layer]).wait()


def unpack_first(src, dst, number, scale):
    channels = dst.shape[1]
    half = 9 * channels // 2
    at = number * channels
    for c in range(2):
        dst[3 * number + c] = (
            src[at : at + channels, c * channels : (c + 1) * channels].astype(F32) * scale
        )
    for low in range(0, channels, channels // 2):
        row = at + low
        part, side = (row, 0) if row < half else (row - half, 1)
        part += 9 * channels
        dst[3 * number + 2, low : low + channels // 2] = (
            src[part : part + channels // 2, side * channels : (side + 1) * channels].astype(F32)
            * scale
        )


def unpack_second(src, dst, number, scale):
    channels = dst.shape[1]
    half = 3 * channels // 2
    place = 8 - number
    for c in range(3):
        if place < 8:
            at = (place // 2) * 3 * channels + c * channels
            side = place % 2
            dst[3 * number + c] = (
                src[at : at + channels, side * channels : (side + 1) * channels].astype(F32)
                * scale
            )
            continue
        for low in range(0, channels, channels // 2):
            row = c * channels + low
            part, side = (row, 0) if row < half else (row - half, 1)
            part += 12 * channels
            dst[3 * number + c, low : low + channels // 2] = (
                src[part : part + channels // 2, side * channels : (side + 1) * channels].astype(
                    F32
                )
                * scale
            )


def unpack_kernel(scale, swap, src, *refs):
    first_o, second_o, buf, sems = refs[-4:]
    core = lax.axis_index("gz") & 1

    def run(unpack, out):
        copies = []
        for depth in range(3):
            for number in range(3 * depth, 3 * depth + 3):
                unpack(src, buf, number, scale)
            part = pl.ds(9 * depth, 9)
            copies.append(pltpu.make_async_copy(buf.at[part], out.at[part], sems.at[depth]))
            copies[-1].start()
        for copy in copies:
            copy.wait()

    @pl.when(core == swap)
    def _():
        run(unpack_first, first_o)

    @pl.when(core == 1 - swap)
    def _():
        run(unpack_second, second_o)


def swapped(array, mask):
    return lax.ppermute(array, "gz", [(i, i ^ mask) for i in range(lax.axis_size("gz"))])


def swapped_chips(array):
    pairs = [(i, i + 1) for i in range(1, lax.axis_size("gz") - 1, 2)]
    return lax.ppermute(array, "gz", pairs + [(j, i) for i, j in pairs])


def picked(stack, i):
    return lax.dynamic_index_in_dim(stack, i, 0, keepdims=False)


def quarter_of(mine, theirs):
    quarter = (lax.axis_index("gz") >> 1) & 3
    stack = (mine + swapped(theirs, 1)).reshape(4, -1, *mine.shape[1:])
    sent = [picked(stack, quarter ^ other).astype(BF16) for other in (1, 2, 3)]
    return picked(stack, quarter), sent


def whole_of(total):
    mask = 16
    while mask < lax.axis_size("gz"):
        total = total + swapped(total, mask)
        mask *= 2
    return total.astype(BF16)


def in_order(found, shape):
    quarter = (lax.axis_index("gz") >> 1) & 3
    stack = jnp.stack(found)
    return jnp.stack([picked(stack, quarter ^ place) for place in range(4)]).reshape(shape)


def shards(volume, cotangent, first_kernel, second_kernel):
    layers, channels, rows, columns = volume.shape
    flat = rows * columns
    wide = flat + 2 * columns
    devices = lax.axis_size("gz")
    conv_flops = 2 * 27 * channels * channels * flat
    layer_bytes = 2 * channels * flat

    def cost(passes, moved):
        return pl.CostEstimate(
            flops=passes * conv_flops, bytes_accessed=moved * layer_bytes, transcendentals=0
        )

    def params():
        return pltpu.CompilerParams(vmem_limit_bytes=LIMIT)

    shape = jax.ShapeDtypeStruct
    edge = jnp.where(lax.axis_index("gz") & 1 == 0, layers - 1, 0)
    near, far = (
        jnp.concatenate(
            [lax.dynamic_slice_in_dim(field, at, 1) for field in (volume, cotangent)], axis=1
        )
        for at in (edge, layers - 1 - edge)
    )
    off_chip = swapped_chips(far)
    on_chip = swapped(near, 1)

    taps = shape((3 * channels, 9 * channels), BF16)
    layer = shape((1, channels, flat), BF16)
    (
        volume_p,
        cot_p,
        inner,
        on_edge,
        first_in,
        second_in,
        part,
        forward,
        adjoint,
        flipped,
    ) = pl.pallas_call(
        inner_kernel,
        out_shape=(
            shape((layers + 2, channels, wide), BF16),
            shape((layers + 2, channels, wide), BF16),
            shape((layers - 2, channels, flat), BF16),
            layer,
            shape((9 * channels, 3 * channels), F32),
            shape((3 * channels, 9 * channels), F32),
            shape((2, 3 * channels, flat), F32),
            taps,
            taps,
            taps,
        ),
        in_specs=[VM] * 5,
        out_specs=(VM,) * 10,
        scratch_shapes=[pltpu.VMEM((2, channels * rows, columns), F32)],
        compiler_params=params(),
        cost_estimate=cost(4 * (layers - 1), 4 * layers),
        name="inner",
    )(volume, cotangent, on_chip, first_kernel, second_kernel)

    packed = shape((27 * channels * channels // 128, 128), F32)
    off_edge, mine, theirs = pl.pallas_call(
        outer_kernel,
        out_shape=(layer, packed, packed),
        in_specs=[VM] * 8,
        out_specs=(VM,) * 3,
        scratch_shapes=[
            pltpu.VMEM((2, 3, channels, wide), BF16),
            pltpu.VMEM((2, channels * rows, columns), F32),
        ],
        compiler_params=params(),
        cost_estimate=cost(4, 8),
        name="outer",
    )(off_chip, volume_p, cot_p, first_in, second_in, part, forward, adjoint)

    tiles = (packed.shape[0] // 8, 8, 128)
    own, sent = quarter_of(mine.reshape(tiles), theirs.reshape(tiles))
    sent, on_edge = lax.optimization_barrier((sent, on_edge))
    total = own
    for other in (1, 2, 3):
        total = total + swapped(sent[other - 1], 2 * other).astype(F32)
    on_chip_g = swapped(on_edge, 1)
    total, off_edge = lax.optimization_barrier((total, off_edge))
    off_chip_g = swapped_chips(off_edge)
    total = total + swapped(total, 8)
    total, flipped = lax.optimization_barrier((whole_of(total), flipped))
    grad_volume = pl.pallas_call(
        volume_kernel,
        out_shape=shape(volume.shape, BF16),
        in_specs=[VM] * 7,
        out_specs=ANY,
        scratch_shapes=[
            pltpu.VMEM((layers + 2, channels, wide), BF16),
            pltpu.VMEM((2, channels * rows, columns), F32),
            pltpu.VMEM(volume.shape, BF16),
            pltpu.SemaphoreType.DMA((layers,)),
        ],
        compiler_params=params(),
        cost_estimate=cost(layers, 4 * layers),
        name="volume",
    )(on_chip_g, off_chip_g, inner, on_edge, off_edge, cotangent, flipped)

    found = [total] + [swapped(total, 2 * other) for other in (1, 2, 3)]
    found, grad_volume = lax.optimization_barrier((found, grad_volume))
    own = in_order(found, tiles)
    other = swapped(own, 1)
    scale = 1.0 / math.sqrt(layers * devices * flat)
    grads = ()
    for swap, part in enumerate((own, other)):
        grads = pl.pallas_call(
            functools.partial(unpack_kernel, scale, swap),
            out_shape=(shape((27, channels, channels), F32),) * 2,
            in_specs=[VM] + [ANY] * len(grads),
            out_specs=(ANY,) * 2,
            scratch_shapes=[
                pltpu.VMEM((27, channels, channels), F32),
                pltpu.SemaphoreType.DMA((3,)),
            ],
            input_output_aliases={1: 0, 2: 1} if grads else {},
            compiler_params=params(),
            cost_estimate=cost(0, 6),
            name="unpack",
        )(part.reshape(packed.shape), *grads)
    first_grad, second_grad = grads
    return grad_volume, first_grad, second_grad


def solution(mesh):
    placed = (
        P(("groups", "gz"), None, None, None),
        P(("groups", "gz"), None, None, None),
        P(),
        P(),
    )
    return jax.shard_map(
        shards,
        mesh=mesh,
        in_specs=placed,
        out_specs=(
            P(("groups", "gz"), None, None, None),
            P("groups", None, None),
            P("groups", None, None),
        ),
        check_vma=False,
    )
```

```python
import functools
import math

import jax
import jax.numpy as jnp
from jax import lax
from jax.experimental import pallas as pl
from jax.experimental.pallas import tpu as pltpu
from jax.sharding import PartitionSpec as P

F32 = jnp.float32
BF16 = jnp.bfloat16
VM = pl.BlockSpec(memory_space=pltpu.VMEM)
ANY = pl.BlockSpec(memory_space=pl.ANY)
LIMIT = 24 << 20


def relayout(src, dst, wide):
    channels, rows, columns = src.shape
    wide[...] = src[...].astype(F32).reshape(channels * rows, columns)
    for row in range(rows):
        dst[:, (row + 1) * columns : (row + 2) * columns] = wide[
            pl.ds(row, channels, stride=rows), :
        ].astype(BF16)


def zero_rows(padded, columns):
    layers, channels, width = padded.shape
    zeros = jnp.zeros((channels, columns), BF16)
    for layer in range(layers):
        padded[layer, :, :columns] = zeros
        padded[layer, :, width - columns :] = zeros


def windows(three, columns, flat):
    return jnp.concatenate(
        [layer[:, b * columns : b * columns + flat] for layer in three for b in range(3)], axis=0
    )


def shifted(field, step, columns):
    channels, flat = field.shape
    lane = lax.broadcasted_iota(jnp.int32, (channels, columns), 1)
    keep = lane != (0 if step == 1 else columns - 1)
    return jnp.concatenate(
        [
            jnp.where(keep, pltpu.roll(field[:, at : at + columns], step % columns, 1), 0.0)
            for at in range(0, flat, columns)
        ],
        axis=1,
    )


def joined(three, step, columns):
    channels = three.shape[0] // 3
    return (
        three[channels : 2 * channels]
        + shifted(three[:channels], step, columns)
        + shifted(three[2 * channels :], -step, columns)
    )


def column_taps(field, step, columns):
    return jnp.concatenate(
        [
            shifted(field, -step, columns).astype(BF16),
            field.astype(BF16),
            shifted(field, step, columns).astype(BF16),
        ],
        axis=0,
    )


def one_layer(near_volume, near_cot, products, columns, flat):
    volume_windows = windows(near_volume, columns, flat)
    cot_windows = windows(near_cot, columns, flat)
    of_volume, of_cot = products(volume_windows, cot_windows)
    hidden = joined(of_volume, 1, columns)
    back_act = joined(of_cot, -1, columns)
    sigmoid_h = jax.nn.sigmoid(hidden)
    activation = (hidden * sigmoid_h).astype(BF16)
    grad_hidden = (back_act * sigmoid_h * (1.0 + hidden * (1.0 - sigmoid_h))).astype(BF16)
    last = (((1,), (1,)), ((), ()))
    first_term = lax.dot_general(
        volume_windows,
        column_taps(grad_hidden.astype(F32), 1, columns),
        last,
        preferred_element_type=F32,
    )
    second_term = lax.dot_general(
        column_taps(activation.astype(F32), -1, columns),
        cot_windows,
        last,
        preferred_element_type=F32,
    )
    return grad_hidden, first_term, second_term


def forward_taps(taps, out):
    for number in range(9):
        channels = taps.shape[1]
        row = jnp.concatenate([taps[3 * number + c].astype(F32) for c in range(3)], axis=1)
        out[:, number * channels : (number + 1) * channels] = row.T.astype(BF16)


def adjoint_taps(taps, out):
    channels = taps.shape[1]
    for c in range(3):
        out[c * channels : (c + 1) * channels, :] = jnp.concatenate(
            [taps[3 * (8 - number) + c] for number in range(9)], axis=1
        )


def inner_kernel(
    volume,
    cot,
    on_chip,
    first_k,
    second_k,
    volume_o,
    cot_o,
    grad_o,
    edge_o,
    first_o,
    second_o,
    part_o,
    forward,
    adjoint,
    flipped,
    wide,
):
    layers, channels, rows, columns = volume.shape
    flat = rows * columns
    forward_taps(first_k, forward)
    adjoint_taps(second_k, adjoint)
    adjoint_taps(first_k, flipped)
    zero_rows(volume_o, columns)
    zero_rows(cot_o, columns)
    core = lax.axis_index("gz") & 1
    rim = (layers + 1) * (1 - core)
    for layer in range(layers):
        relayout(volume.at[layer], volume_o.at[layer + 1], wide.at[0])
        relayout(cot.at[layer], cot_o.at[layer + 1], wide.at[1])
    relayout(on_chip.at[0, pl.ds(0, channels)], volume_o.at[rim], wide.at[0])
    relayout(on_chip.at[0, pl.ds(channels, channels)], cot_o.at[rim], wide.at[1])
    edge = 1 + (layers - 1) * (1 - core)

    def products(volume_windows, cot_windows):
        return (
            jnp.dot(forward[...], volume_windows, preferred_element_type=F32),
            jnp.dot(adjoint[...], cot_windows, preferred_element_type=F32),
        )

    for place, layer in enumerate([*range(2, layers), edge]):
        grad_hidden, first_term, second_term = one_layer(
            [volume_o[layer + a] for a in (-1, 0, 1)],
            [cot_o[layer + a] for a in (-1, 0, 1)],
            products,
            columns,
            flat,
        )
        if place < layers - 2:
            grad_o[place] = grad_hidden
        else:
            edge_o[0] = grad_hidden
        if place == 0:
            first_o[...] = first_term
            second_o[...] = second_term
        else:
            first_o[...] += first_term
            second_o[...] += second_term

    layer = 1 + (layers - 1) * core
    for padded in (volume_o, cot_o):
        padded[(layers + 1) * core] = jnp.zeros(padded.shape[1:], BF16)
    part_o[0], part_o[1] = products(
        windows([volume_o[layer + a] for a in (-1, 0, 1)], columns, flat),
        windows([cot_o[layer + a] for a in (-1, 0, 1)], columns, flat),
    )


def pack_first(term):
    half = term.shape[0] // 2
    return term[:, :128], jnp.concatenate([term[:half, 128:], term[half:, 128:]], axis=1)


def pack_second(term):
    half = term.shape[0] // 2
    pieces = [term[:, at : at + 128] for at in range(0, 512, 128)]
    return pieces + [jnp.concatenate([term[:half, 512:], term[half:, 512:]], axis=1)]


def put_rows(dst, pieces):
    at = 0
    for piece in pieces:
        dst[at : at + piece.shape[0], :] = piece
        at += piece.shape[0]


def outer_kernel(
    off_chip,
    volume_p,
    cot_p,
    first_in,
    second_in,
    part,
    forward,
    adjoint,
    edge_o,
    mine_o,
    theirs_o,
    near,
    wide,
):
    layers = volume_p.shape[0] - 2
    channels = off_chip.shape[1] // 2
    rows, columns = off_chip.shape[2:]
    flat = rows * columns
    core = lax.axis_index("gz") & 1
    edge = 1 + (layers - 1) * core
    for kind, padded in enumerate((volume_p, cot_p)):
        rim = near.at[kind, 2 * core]
        zeros = jnp.zeros((channels, columns), BF16)
        rim[:, :columns] = zeros
        rim[:, columns + flat :] = zeros
        relayout(off_chip.at[0, pl.ds(kind * channels, channels)], rim, wide.at[kind])
        near[kind, 1] = padded[edge]
        near[kind, 2 - 2 * core] = padded[edge + 1 - 2 * core]
    depth = 3 * channels
    beyond = pl.ds(pl.multiple_of(2 * depth * core, 128), depth)

    def products(*unused):
        return [
            part[kind]
            + jnp.dot(
                taps[:, beyond],
                jnp.concatenate(
                    [near[kind, 2 * core, :, pl.ds(b * columns, flat)] for b in range(3)], axis=0
                ),
                preferred_element_type=F32,
            )
            for kind, taps in enumerate((forward, adjoint))
        ]

    grad_hidden, first_term, second_term = one_layer(
        [near[0, a] for a in range(3)],
        [near[1, a] for a in range(3)],
        products,
        columns,
        flat,
    )
    edge_o[0] = grad_hidden
    first = pack_first(first_in[...] + first_term)
    second = pack_second(second_in[...] + second_term)

    @pl.when(core == 0)
    def _():
        put_rows(mine_o, first)
        put_rows(theirs_o, second)

    @pl.when(core == 1)
    def _():
        put_rows(mine_o, second)
        put_rows(theirs_o, first)


def volume_kernel(
    on_chip, off_chip, inner, on_edge, off_edge, cot, adjoint, out, padded, wide, buf, out_sem
):
    layers, channels, rows, columns = cot.shape
    flat = rows * columns
    core = lax.axis_index("gz") & 1
    zero_rows(padded, columns)
    middle = slice(columns, columns + flat)
    padded[(1 - core) * (layers + 1), :, middle] = on_chip[0]
    padded[core * (layers + 1), :, middle] = off_chip[0]
    padded[1 + (layers - 1) * (1 - core), :, middle] = on_edge[0]
    padded[1 + (layers - 1) * core, :, middle] = off_edge[0]
    for layer in range(layers - 2):
        padded[layer + 2, :, middle] = inner[layer]
    for layer in range(layers):
        three = jnp.dot(
            adjoint[...],
            windows([padded[layer + a] for a in range(3)], columns, flat),
            preferred_element_type=F32,
        )
        summed = joined(three, -1, columns)
        scratch = wide.at[layer % 2]
        for row in range(rows):
            scratch[pl.ds(row, channels, stride=rows), :] = summed[
                :, row * columns : (row + 1) * columns
            ]
        buf[layer] = (
            cot[layer].astype(F32) + scratch[...].reshape(channels, rows, columns)
        ).astype(BF16)
        pltpu.make_async_copy(buf.at[layer], out.at[layer], out_sem.at[layer]).start()
    for layer in range(layers):
        pltpu.make_async_copy(buf.at[layer], out.at[layer], out_sem.at[layer]).wait()


def unpack_first(src, dst, number, scale):
    channels = dst.shape[1]
    half = 9 * channels // 2
    at = number * channels
    for c in range(2):
        dst[3 * number + c] = (
            src[at : at + channels, c * channels : (c + 1) * channels].astype(F32) * scale
        )
    for low in range(0, channels, channels // 2):
        row = at + low
        part, side = (row, 0) if row < half else (row - half, 1)
        part += 9 * channels
        dst[3 * number + 2, low : low + channels // 2] = (
            src[part : part + channels // 2, side * channels : (side + 1) * channels].astype(F32)
            * scale
        )


def unpack_second(src, dst, number, scale):
    channels = dst.shape[1]
    half = 3 * channels // 2
    place = 8 - number
    for c in range(3):
        if place < 8:
            at = (place // 2) * 3 * channels + c * channels
            side = place % 2
            dst[3 * number + c] = (
                src[at : at + channels, side * channels : (side + 1) * channels].astype(F32)
                * scale
            )
            continue
        for low in range(0, channels, channels // 2):
            row = c * channels + low
            part, side = (row, 0) if row < half else (row - half, 1)
            part += 12 * channels
            dst[3 * number + c, low : low + channels // 2] = (
                src[part : part + channels // 2, side * channels : (side + 1) * channels].astype(
                    F32
                )
                * scale
            )


def unpack_kernel(scale, swap, src, *refs):
    first_o, second_o, buf, sems = refs[-4:]
    core = lax.axis_index("gz") & 1

    def run(unpack, out):
        copies = []
        for depth in range(3):
            for number in range(3 * depth, 3 * depth + 3):
                unpack(src, buf, number, scale)
            part = pl.ds(9 * depth, 9)
            copies.append(pltpu.make_async_copy(buf.at[part], out.at[part], sems.at[depth]))
            copies[-1].start()
        for copy in copies:
            copy.wait()

    @pl.when(core == swap)
    def _():
        run(unpack_first, first_o)

    @pl.when(core == 1 - swap)
    def _():
        run(unpack_second, second_o)


def swapped(array, mask):
    return lax.ppermute(array, "gz", [(i, i ^ mask) for i in range(lax.axis_size("gz"))])


def swapped_chips(array):
    pairs = [(i, i + 1) for i in range(1, lax.axis_size("gz") - 1, 2)]
    return lax.ppermute(array, "gz", pairs + [(j, i) for i, j in pairs])


def picked(stack, i):
    return lax.dynamic_index_in_dim(stack, i, 0, keepdims=False)


def quarter_of(mine, theirs):
    quarter = (lax.axis_index("gz") >> 1) & 3
    stack = (mine + swapped(theirs, 1)).reshape(4, -1, *mine.shape[1:])
    sent = [picked(stack, quarter ^ other).astype(BF16) for other in (1, 2, 3)]
    return picked(stack, quarter), sent


def rounded(array):
    top = jnp.max(jnp.abs(array), axis=0, keepdims=True)
    power = jnp.maximum(jnp.ceil(jnp.log2(top)), -100.0)
    return jnp.concatenate(
        [(array * jnp.exp2(14.0 - power)).astype(jnp.float16), power.astype(jnp.float16)]
    )


def widened(coded):
    return coded[:-1].astype(F32) * jnp.exp2(coded[-1:].astype(F32) - 14.0)


def whole_of(total):
    mask = 16
    while mask < lax.axis_size("gz"):
        total = total + swapped(total, mask)
        mask *= 2
    return total.astype(BF16)


def in_order(found, shape):
    quarter = (lax.axis_index("gz") >> 1) & 3
    stack = jnp.stack(found)
    return jnp.stack([picked(stack, quarter ^ place) for place in range(4)]).reshape(shape)


def shards(volume, cotangent, first_kernel, second_kernel):
    layers, channels, rows, columns = volume.shape
    flat = rows * columns
    wide = flat + 2 * columns
    devices = lax.axis_size("gz")
    conv_flops = 2 * 27 * channels * channels * flat
    layer_bytes = 2 * channels * flat

    def cost(passes, moved):
        return pl.CostEstimate(
            flops=passes * conv_flops, bytes_accessed=moved * layer_bytes, transcendentals=0
        )

    def params():
        return pltpu.CompilerParams(vmem_limit_bytes=LIMIT)

    shape = jax.ShapeDtypeStruct
    edge = jnp.where(lax.axis_index("gz") & 1 == 0, layers - 1, 0)
    near, far = (
        jnp.concatenate(
            [lax.dynamic_slice_in_dim(field, at, 1) for field in (volume, cotangent)], axis=1
        )
        for at in (edge, layers - 1 - edge)
    )
    off_chip = swapped_chips(far)
    on_chip = swapped(near, 1)

    taps = shape((3 * channels, 9 * channels), BF16)
    layer = shape((1, channels, flat), BF16)
    (
        volume_p,
        cot_p,
        inner,
        on_edge,
        first_in,
        second_in,
        part,
        forward,
        adjoint,
        flipped,
    ) = pl.pallas_call(
        inner_kernel,
        out_shape=(
            shape((layers + 2, channels, wide), BF16),
            shape((layers + 2, channels, wide), BF16),
            shape((layers - 2, channels, flat), BF16),
            layer,
            shape((9 * channels, 3 * channels), F32),
            shape((3 * channels, 9 * channels), F32),
            shape((2, 3 * channels, flat), F32),
            taps,
            taps,
            taps,
        ),
        in_specs=[VM] * 5,
        out_specs=(VM,) * 10,
        scratch_shapes=[pltpu.VMEM((2, channels * rows, columns), F32)],
        compiler_params=params(),
        cost_estimate=cost(4 * (layers - 1), 4 * layers),
        name="inner",
    )(volume, cotangent, on_chip, first_kernel, second_kernel)

    packed = shape((27 * channels * channels // 128, 128), F32)
    off_edge, mine, theirs = pl.pallas_call(
        outer_kernel,
        out_shape=(layer, packed, packed),
        in_specs=[VM] * 8,
        out_specs=(VM,) * 3,
        scratch_shapes=[
            pltpu.VMEM((2, 3, channels, wide), BF16),
            pltpu.VMEM((2, channels * rows, columns), F32),
        ],
        compiler_params=params(),
        cost_estimate=cost(4, 8),
        name="outer",
    )(off_chip, volume_p, cot_p, first_in, second_in, part, forward, adjoint)

    tiles = (packed.shape[0] // 8, 8, 128)
    own, sent = quarter_of(mine.reshape(tiles), theirs.reshape(tiles))
    sent, on_edge = lax.optimization_barrier((sent, on_edge))
    total = own
    for other in (1, 2, 3):
        total = total + swapped(sent[other - 1], 2 * other).astype(F32)
    on_chip_g = swapped(on_edge, 1)
    coded = rounded(total)
    coded, off_edge = lax.optimization_barrier((coded, off_edge))
    off_chip_g = swapped_chips(off_edge)
    total = widened(coded) + widened(swapped(coded, 8))
    total, flipped = lax.optimization_barrier((whole_of(total), flipped))
    grad_volume = pl.pallas_call(
        volume_kernel,
        out_shape=shape(volume.shape, BF16),
        in_specs=[VM] * 7,
        out_specs=ANY,
        scratch_shapes=[
            pltpu.VMEM((layers + 2, channels, wide), BF16),
            pltpu.VMEM((2, channels * rows, columns), F32),
            pltpu.VMEM(volume.shape, BF16),
            pltpu.SemaphoreType.DMA((layers,)),
        ],
        compiler_params=params(),
        cost_estimate=cost(layers, 4 * layers),
        name="volume",
    )(on_chip_g, off_chip_g, inner, on_edge, off_edge, cotangent, flipped)

    found = [total] + [swapped(total, 2 * other) for other in (1, 2, 3)]
    found, grad_volume = lax.optimization_barrier((found, grad_volume))
    own = in_order(found, tiles)
    other = swapped(own, 1)
    scale = 1.0 / math.sqrt(layers * devices * flat)
    grads = ()
    for swap, part in enumerate((own, other)):
        grads = pl.pallas_call(
            functools.partial(unpack_kernel, scale, swap),
            out_shape=(shape((27, channels, channels), F32),) * 2,
            in_specs=[VM] + [ANY] * len(grads),
            out_specs=(ANY,) * 2,
            scratch_shapes=[
                pltpu.VMEM((27, channels, channels), F32),
                pltpu.SemaphoreType.DMA((3,)),
            ],
            input_output_aliases={1: 0, 2: 1} if grads else {},
            compiler_params=params(),
            cost_estimate=cost(0, 6),
            name="unpack",
        )(part.reshape(packed.shape), *grads)
    first_grad, second_grad = grads
    return grad_volume, first_grad, second_grad


def solution(mesh):
    placed = (
        P(("groups", "gz"), None, None, None),
        P(("groups", "gz"), None, None, None),
        P(),
        P(),
    )
    return jax.shard_map(
        shards,
        mesh=mesh,
        in_specs=placed,
        out_specs=(
            P(("groups", "gz"), None, None, None),
            P("groups", None, None),
            P("groups", None, None),
        ),
        check_vma=False,
    )
```

```python
import functools
import math

import jax
import jax.numpy as jnp
from jax import lax
from jax.experimental import pallas as pl
from jax.experimental.pallas import tpu as pltpu
from jax.sharding import PartitionSpec as P

F32 = jnp.float32
BF16 = jnp.bfloat16
VM = pl.BlockSpec(memory_space=pltpu.VMEM)
ANY = pl.BlockSpec(memory_space=pl.ANY)
LIMIT = 24 << 20


def relayout(src, dst, wide):
    channels, rows, columns = src.shape
    wide[...] = src[...].astype(F32).reshape(channels * rows, columns)
    for row in range(rows):
        dst[:, (row + 1) * columns : (row + 2) * columns] = wide[
            pl.ds(row, channels, stride=rows), :
        ].astype(BF16)


def zero_rows(padded, columns):
    layers, channels, width = padded.shape
    zeros = jnp.zeros((channels, columns), BF16)
    for layer in range(layers):
        padded[layer, :, :columns] = zeros
        padded[layer, :, width - columns :] = zeros


def windows(three, columns, flat):
    return jnp.concatenate(
        [layer[:, b * columns : b * columns + flat] for layer in three for b in range(3)], axis=0
    )


def shifted(field, step, columns):
    channels, flat = field.shape
    lane = lax.broadcasted_iota(jnp.int32, (channels, columns), 1)
    keep = lane != (0 if step == 1 else columns - 1)
    return jnp.concatenate(
        [
            jnp.where(keep, pltpu.roll(field[:, at : at + columns], step % columns, 1), 0.0)
            for at in range(0, flat, columns)
        ],
        axis=1,
    )


def joined(three, step, columns):
    channels = three.shape[0] // 3
    return (
        three[channels : 2 * channels]
        + shifted(three[:channels], step, columns)
        + shifted(three[2 * channels :], -step, columns)
    )


def column_taps(field, step, columns):
    return jnp.concatenate(
        [
            shifted(field, -step, columns).astype(BF16),
            field.astype(BF16),
            shifted(field, step, columns).astype(BF16),
        ],
        axis=0,
    )


def one_layer(near_volume, near_cot, products, columns, flat):
    volume_windows = windows(near_volume, columns, flat)
    cot_windows = windows(near_cot, columns, flat)
    of_volume, of_cot = products(volume_windows, cot_windows)
    hidden = joined(of_volume, 1, columns)
    back_act = joined(of_cot, -1, columns)
    sigmoid_h = jax.nn.sigmoid(hidden)
    activation = (hidden * sigmoid_h).astype(BF16)
    grad_hidden = (back_act * sigmoid_h * (1.0 + hidden * (1.0 - sigmoid_h))).astype(BF16)
    last = (((1,), (1,)), ((), ()))
    first_term = lax.dot_general(
        volume_windows,
        column_taps(grad_hidden.astype(F32), 1, columns),
        last,
        preferred_element_type=F32,
    )
    second_term = lax.dot_general(
        column_taps(activation.astype(F32), -1, columns),
        cot_windows,
        last,
        preferred_element_type=F32,
    )
    return grad_hidden, first_term, second_term


def forward_taps(taps, out):
    for number in range(9):
        channels = taps.shape[1]
        row = jnp.concatenate([taps[3 * number + c].astype(F32) for c in range(3)], axis=1)
        out[:, number * channels : (number + 1) * channels] = row.T.astype(BF16)


def adjoint_taps(taps, out):
    channels = taps.shape[1]
    for c in range(3):
        out[c * channels : (c + 1) * channels, :] = jnp.concatenate(
            [taps[3 * (8 - number) + c] for number in range(9)], axis=1
        )


def inner_kernel(
    volume,
    cot,
    on_chip,
    first_k,
    second_k,
    volume_o,
    cot_o,
    grad_o,
    edge_o,
    first_o,
    second_o,
    part_o,
    forward,
    adjoint,
    flipped,
    wide,
):
    layers, channels, rows, columns = volume.shape
    flat = rows * columns
    forward_taps(first_k, forward)
    adjoint_taps(second_k, adjoint)
    adjoint_taps(first_k, flipped)
    zero_rows(volume_o, columns)
    zero_rows(cot_o, columns)
    core = lax.axis_index("gz") & 1
    rim = (layers + 1) * (1 - core)
    for layer in range(layers):
        relayout(volume.at[layer], volume_o.at[layer + 1], wide.at[0])
        relayout(cot.at[layer], cot_o.at[layer + 1], wide.at[1])
    relayout(on_chip.at[0, pl.ds(0, channels)], volume_o.at[rim], wide.at[0])
    relayout(on_chip.at[0, pl.ds(channels, channels)], cot_o.at[rim], wide.at[1])
    edge = 1 + (layers - 1) * (1 - core)

    def products(volume_windows, cot_windows):
        return (
            jnp.dot(forward[...], volume_windows, preferred_element_type=F32),
            jnp.dot(adjoint[...], cot_windows, preferred_element_type=F32),
        )

    for place, layer in enumerate([*range(2, layers), edge]):
        grad_hidden, first_term, second_term = one_layer(
            [volume_o[layer + a] for a in (-1, 0, 1)],
            [cot_o[layer + a] for a in (-1, 0, 1)],
            products,
            columns,
            flat,
        )
        if place < layers - 2:
            grad_o[place] = grad_hidden
        else:
            edge_o[0] = grad_hidden
        if place == 0:
            first_o[...] = first_term
            second_o[...] = second_term
        else:
            first_o[...] += first_term
            second_o[...] += second_term

    layer = 1 + (layers - 1) * core
    for padded in (volume_o, cot_o):
        padded[(layers + 1) * core] = jnp.zeros(padded.shape[1:], BF16)
    part_o[0], part_o[1] = products(
        windows([volume_o[layer + a] for a in (-1, 0, 1)], columns, flat),
        windows([cot_o[layer + a] for a in (-1, 0, 1)], columns, flat),
    )


def pack_first(term):
    half = term.shape[0] // 2
    return term[:, :128], jnp.concatenate([term[:half, 128:], term[half:, 128:]], axis=1)


def pack_second(term):
    half = term.shape[0] // 2
    pieces = [term[:, at : at + 128] for at in range(0, 512, 128)]
    return pieces + [jnp.concatenate([term[:half, 512:], term[half:, 512:]], axis=1)]


def put_rows(dst, pieces):
    at = 0
    for piece in pieces:
        dst[at : at + piece.shape[0], :] = piece
        at += piece.shape[0]


def outer_kernel(
    off_chip,
    volume_p,
    cot_p,
    first_in,
    second_in,
    part,
    forward,
    adjoint,
    edge_o,
    mine_o,
    theirs_o,
    near,
    wide,
):
    layers = volume_p.shape[0] - 2
    channels = off_chip.shape[1] // 2
    rows, columns = off_chip.shape[2:]
    flat = rows * columns
    core = lax.axis_index("gz") & 1
    edge = 1 + (layers - 1) * core
    for kind, padded in enumerate((volume_p, cot_p)):
        rim = near.at[kind, 2 * core]
        zeros = jnp.zeros((channels, columns), BF16)
        rim[:, :columns] = zeros
        rim[:, columns + flat :] = zeros
        relayout(off_chip.at[0, pl.ds(kind * channels, channels)], rim, wide.at[kind])
        near[kind, 1] = padded[edge]
        near[kind, 2 - 2 * core] = padded[edge + 1 - 2 * core]
    depth = 3 * channels
    beyond = pl.ds(pl.multiple_of(2 * depth * core, 128), depth)

    def products(*unused):
        return [
            part[kind]
            + jnp.dot(
                taps[:, beyond],
                jnp.concatenate(
                    [near[kind, 2 * core, :, pl.ds(b * columns, flat)] for b in range(3)], axis=0
                ),
                preferred_element_type=F32,
            )
            for kind, taps in enumerate((forward, adjoint))
        ]

    grad_hidden, first_term, second_term = one_layer(
        [near[0, a] for a in range(3)],
        [near[1, a] for a in range(3)],
        products,
        columns,
        flat,
    )
    edge_o[0] = grad_hidden
    first = pack_first(first_in[...] + first_term)
    second = pack_second(second_in[...] + second_term)

    @pl.when(core == 0)
    def _():
        put_rows(mine_o, first)
        put_rows(theirs_o, second)

    @pl.when(core == 1)
    def _():
        put_rows(mine_o, second)
        put_rows(theirs_o, first)


def volume_kernel(
    on_chip, off_chip, inner, on_edge, off_edge, cot, adjoint, out, padded, wide, buf, out_sem
):
    layers, channels, rows, columns = cot.shape
    flat = rows * columns
    core = lax.axis_index("gz") & 1
    zero_rows(padded, columns)
    middle = slice(columns, columns + flat)
    padded[(1 - core) * (layers + 1), :, middle] = on_chip[0]
    padded[core * (layers + 1), :, middle] = off_chip[0]
    padded[1 + (layers - 1) * (1 - core), :, middle] = on_edge[0]
    padded[1 + (layers - 1) * core, :, middle] = off_edge[0]
    for layer in range(layers - 2):
        padded[layer + 2, :, middle] = inner[layer]
    for layer in range(layers):
        three = jnp.dot(
            adjoint[...],
            windows([padded[layer + a] for a in range(3)], columns, flat),
            preferred_element_type=F32,
        )
        summed = joined(three, -1, columns)
        scratch = wide.at[layer % 2]
        for row in range(rows):
            scratch[pl.ds(row, channels, stride=rows), :] = summed[
                :, row * columns : (row + 1) * columns
            ]
        buf[layer] = (
            cot[layer].astype(F32) + scratch[...].reshape(channels, rows, columns)
        ).astype(BF16)
        pltpu.make_async_copy(buf.at[layer], out.at[layer], out_sem.at[layer]).start()
    for layer in range(layers):
        pltpu.make_async_copy(buf.at[layer], out.at[layer], out_sem.at[layer]).wait()


def unpack_first(src, dst, number, scale):
    channels = dst.shape[1]
    half = 9 * channels // 2
    at = number * channels
    for c in range(2):
        dst[3 * number + c] = (
            src[at : at + channels, c * channels : (c + 1) * channels].astype(F32) * scale
        )
    for low in range(0, channels, channels // 2):
        row = at + low
        part, side = (row, 0) if row < half else (row - half, 1)
        part += 9 * channels
        dst[3 * number + 2, low : low + channels // 2] = (
            src[part : part + channels // 2, side * channels : (side + 1) * channels].astype(F32)
            * scale
        )


def unpack_second(src, dst, number, scale):
    channels = dst.shape[1]
    half = 3 * channels // 2
    place = 8 - number
    for c in range(3):
        if place < 8:
            at = (place // 2) * 3 * channels + c * channels
            side = place % 2
            dst[3 * number + c] = (
                src[at : at + channels, side * channels : (side + 1) * channels].astype(F32)
                * scale
            )
            continue
        for low in range(0, channels, channels // 2):
            row = c * channels + low
            part, side = (row, 0) if row < half else (row - half, 1)
            part += 12 * channels
            dst[3 * number + c, low : low + channels // 2] = (
                src[part : part + channels // 2, side * channels : (side + 1) * channels].astype(
                    F32
                )
                * scale
            )


def unpack_kernel(scale, swap, src, *refs):
    first_o, second_o, buf, sems = refs[-4:]
    core = lax.axis_index("gz") & 1

    def run(unpack, out):
        copies = []
        for depth in range(3):
            for number in range(3 * depth, 3 * depth + 3):
                unpack(src, buf, number, scale)
            part = pl.ds(9 * depth, 9)
            copies.append(pltpu.make_async_copy(buf.at[part], out.at[part], sems.at[depth]))
            copies[-1].start()
        for copy in copies:
            copy.wait()

    @pl.when(core == swap)
    def _():
        run(unpack_first, first_o)

    @pl.when(core == 1 - swap)
    def _():
        run(unpack_second, second_o)


def swapped(array, mask):
    return lax.ppermute(array, "gz", [(i, i ^ mask) for i in range(lax.axis_size("gz"))])


def swapped_chips(array):
    pairs = [(i, i + 1) for i in range(1, lax.axis_size("gz") - 1, 2)]
    return lax.ppermute(array, "gz", pairs + [(j, i) for i, j in pairs])


def picked(stack, i):
    return lax.dynamic_index_in_dim(stack, i, 0, keepdims=False)


def quarter_of(mine, theirs):
    quarter = (lax.axis_index("gz") >> 1) & 3
    stack = (mine + swapped(theirs, 1)).reshape(4, -1, *mine.shape[1:])
    sent = [picked(stack, quarter ^ other).astype(BF16) for other in (1, 2, 3)]
    return picked(stack, quarter), sent


def rounded(array):
    top = jnp.max(jnp.abs(array), axis=0, keepdims=True)
    power = jnp.maximum(jnp.ceil(jnp.log2(top)), -100.0)
    return jnp.concatenate(
        [(array * jnp.exp2(14.0 - power)).astype(jnp.float16), power.astype(jnp.float16)]
    )


def widened(coded):
    return coded[:-1].astype(F32) * jnp.exp2(coded[-1:].astype(F32) - 14.0)


def whole_of(total):
    mask = 16
    while mask < lax.axis_size("gz"):
        total = total + swapped(total, mask)
        mask *= 2
    return total.astype(BF16)


def in_order(found, shape):
    quarter = (lax.axis_index("gz") >> 1) & 3
    stack = jnp.stack(found)
    order = [quarter ^ place for place in range(4)]
    return jnp.stack(
        [picked(stack, jnp.where(other == 0, 0, other % 3 + 1)) for other in order]
    ).reshape(shape)


def shards(volume, cotangent, first_kernel, second_kernel):
    layers, channels, rows, columns = volume.shape
    flat = rows * columns
    wide = flat + 2 * columns
    devices = lax.axis_size("gz")
    conv_flops = 2 * 27 * channels * channels * flat
    layer_bytes = 2 * channels * flat

    def cost(passes, moved):
        return pl.CostEstimate(
            flops=passes * conv_flops, bytes_accessed=moved * layer_bytes, transcendentals=0
        )

    def params():
        return pltpu.CompilerParams(vmem_limit_bytes=LIMIT)

    shape = jax.ShapeDtypeStruct
    edge = jnp.where(lax.axis_index("gz") & 1 == 0, layers - 1, 0)
    near, far = (
        jnp.concatenate(
            [lax.dynamic_slice_in_dim(field, at, 1) for field in (volume, cotangent)], axis=1
        )
        for at in (edge, layers - 1 - edge)
    )
    off_chip = swapped_chips(far)
    on_chip = swapped(near, 1)

    taps = shape((3 * channels, 9 * channels), BF16)
    layer = shape((1, channels, flat), BF16)
    (
        volume_p,
        cot_p,
        inner,
        on_edge,
        first_in,
        second_in,
        part,
        forward,
        adjoint,
        flipped,
    ) = pl.pallas_call(
        inner_kernel,
        out_shape=(
            shape((layers + 2, channels, wide), BF16),
            shape((layers + 2, channels, wide), BF16),
            shape((layers - 2, channels, flat), BF16),
            layer,
            shape((9 * channels, 3 * channels), F32),
            shape((3 * channels, 9 * channels), F32),
            shape((2, 3 * channels, flat), F32),
            taps,
            taps,
            taps,
        ),
        in_specs=[VM] * 5,
        out_specs=(VM,) * 10,
        scratch_shapes=[pltpu.VMEM((2, channels * rows, columns), F32)],
        compiler_params=params(),
        cost_estimate=cost(4 * (layers - 1), 4 * layers),
        name="inner",
    )(volume, cotangent, on_chip, first_kernel, second_kernel)

    packed = shape((27 * channels * channels // 128, 128), F32)
    off_edge, mine, theirs = pl.pallas_call(
        outer_kernel,
        out_shape=(layer, packed, packed),
        in_specs=[VM] * 8,
        out_specs=(VM,) * 3,
        scratch_shapes=[
            pltpu.VMEM((2, 3, channels, wide), BF16),
            pltpu.VMEM((2, channels * rows, columns), F32),
        ],
        compiler_params=params(),
        cost_estimate=cost(4, 8),
        name="outer",
    )(off_chip, volume_p, cot_p, first_in, second_in, part, forward, adjoint)

    tiles = (packed.shape[0] // 8, 8, 128)
    own, sent = quarter_of(mine.reshape(tiles), theirs.reshape(tiles))
    sent, on_edge = lax.optimization_barrier((sent, on_edge))
    total = own
    for other in (3, 1, 2):
        total = total + swapped(sent[other - 1], 2 * other).astype(F32)
    on_chip_g = swapped(on_edge, 1)
    coded = rounded(total)
    coded, off_edge = lax.optimization_barrier((coded, off_edge))
    off_chip_g = swapped_chips(off_edge)
    total = widened(coded) + widened(swapped(coded, 8))
    total, flipped = lax.optimization_barrier((whole_of(total), flipped))
    grad_volume = pl.pallas_call(
        volume_kernel,
        out_shape=shape(volume.shape, BF16),
        in_specs=[VM] * 7,
        out_specs=ANY,
        scratch_shapes=[
            pltpu.VMEM((layers + 2, channels, wide), BF16),
            pltpu.VMEM((2, channels * rows, columns), F32),
            pltpu.VMEM(volume.shape, BF16),
            pltpu.SemaphoreType.DMA((layers,)),
        ],
        compiler_params=params(),
        cost_estimate=cost(layers, 4 * layers),
        name="volume",
    )(on_chip_g, off_chip_g, inner, on_edge, off_edge, cotangent, flipped)

    found = [total] + [swapped(total, 2 * other) for other in (3, 1, 2)]
    found, grad_volume = lax.optimization_barrier((found, grad_volume))
    own = in_order(found, tiles)
    other = swapped(own, 1)
    scale = 1.0 / math.sqrt(layers * devices * flat)
    grads = ()
    for swap, part in enumerate((own, other)):
        grads = pl.pallas_call(
            functools.partial(unpack_kernel, scale, swap),
            out_shape=(shape((27, channels, channels), F32),) * 2,
            in_specs=[VM] + [ANY] * len(grads),
            out_specs=(ANY,) * 2,
            scratch_shapes=[
                pltpu.VMEM((27, channels, channels), F32),
                pltpu.SemaphoreType.DMA((3,)),
            ],
            input_output_aliases={1: 0, 2: 1} if grads else {},
            compiler_params=params(),
            cost_estimate=cost(0, 6),
            name="unpack",
        )(part.reshape(packed.shape), *grads)
    first_grad, second_grad = grads
    return grad_volume, first_grad, second_grad


def solution(mesh):
    placed = (
        P(("groups", "gz"), None, None, None),
        P(("groups", "gz"), None, None, None),
        P(),
        P(),
    )
    return jax.shard_map(
        shards,
        mesh=mesh,
        in_specs=placed,
        out_specs=(
            P(("groups", "gz"), None, None, None),
            P("groups", None, None),
            P("groups", None, None),
        ),
        check_vma=False,
    )
```

```python
import functools
import math

import jax
import jax.numpy as jnp
from jax import lax
from jax.experimental import pallas as pl
from jax.experimental.pallas import tpu as pltpu
from jax.sharding import PartitionSpec as P

F32 = jnp.float32
BF16 = jnp.bfloat16
VM = pl.BlockSpec(memory_space=pltpu.VMEM)
ANY = pl.BlockSpec(memory_space=pl.ANY)
LIMIT = 24 << 20


def relayout(src, dst, wide):
    channels, rows, columns = src.shape
    wide[...] = src[...].astype(F32).reshape(channels * rows, columns)
    for row in range(rows):
        dst[:, (row + 1) * columns : (row + 2) * columns] = wide[
            pl.ds(row, channels, stride=rows), :
        ].astype(BF16)


def zero_rows(padded, columns):
    layers, channels, width = padded.shape
    zeros = jnp.zeros((channels, columns), BF16)
    for layer in range(layers):
        padded[layer, :, :columns] = zeros
        padded[layer, :, width - columns :] = zeros


def windows(three, columns, flat):
    return jnp.concatenate(
        [layer[:, b * columns : b * columns + flat] for layer in three for b in range(3)], axis=0
    )


def shifted(field, step, columns):
    channels, flat = field.shape
    lane = lax.broadcasted_iota(jnp.int32, (channels, columns), 1)
    keep = lane != (0 if step == 1 else columns - 1)
    return jnp.concatenate(
        [
            jnp.where(keep, pltpu.roll(field[:, at : at + columns], step % columns, 1), 0.0)
            for at in range(0, flat, columns)
        ],
        axis=1,
    )


def joined(three, step, columns):
    channels = three.shape[0] // 3
    return (
        three[channels : 2 * channels]
        + shifted(three[:channels], step, columns)
        + shifted(three[2 * channels :], -step, columns)
    )


def column_taps(field, step, columns):
    return jnp.concatenate(
        [
            shifted(field, -step, columns).astype(BF16),
            field.astype(BF16),
            shifted(field, step, columns).astype(BF16),
        ],
        axis=0,
    )


def one_layer(near_volume, near_cot, products, columns, flat):
    volume_windows = windows(near_volume, columns, flat)
    cot_windows = windows(near_cot, columns, flat)
    of_volume, of_cot = products(volume_windows, cot_windows)
    hidden = joined(of_volume, 1, columns)
    back_act = joined(of_cot, -1, columns)
    sigmoid_h = jax.nn.sigmoid(hidden)
    activation = (hidden * sigmoid_h).astype(BF16)
    grad_hidden = (back_act * sigmoid_h * (1.0 + hidden * (1.0 - sigmoid_h))).astype(BF16)
    last = (((1,), (1,)), ((), ()))
    first_term = lax.dot_general(
        volume_windows,
        column_taps(grad_hidden.astype(F32), 1, columns),
        last,
        preferred_element_type=F32,
    )
    second_term = lax.dot_general(
        column_taps(activation.astype(F32), -1, columns),
        cot_windows,
        last,
        preferred_element_type=F32,
    )
    return grad_hidden, first_term, second_term


def forward_taps(taps, out):
    for number in range(9):
        channels = taps.shape[1]
        row = jnp.concatenate([taps[3 * number + c].astype(F32) for c in range(3)], axis=1)
        out[:, number * channels : (number + 1) * channels] = row.T.astype(BF16)


def adjoint_taps(taps, out):
    channels = taps.shape[1]
    for c in range(3):
        out[c * channels : (c + 1) * channels, :] = jnp.concatenate(
            [taps[3 * (8 - number) + c] for number in range(9)], axis=1
        )


def inner_kernel(
    volume,
    cot,
    on_chip,
    first_k,
    second_k,
    volume_o,
    cot_o,
    grad_o,
    edge_o,
    first_o,
    second_o,
    part_o,
    forward,
    adjoint,
    flipped,
    wide,
):
    layers, channels, rows, columns = volume.shape
    flat = rows * columns
    forward_taps(first_k, forward)
    adjoint_taps(second_k, adjoint)
    adjoint_taps(first_k, flipped)
    zero_rows(volume_o, columns)
    zero_rows(cot_o, columns)
    core = lax.axis_index("gz") & 1
    rim = (layers + 1) * (1 - core)
    for layer in range(layers):
        relayout(volume.at[layer], volume_o.at[layer + 1], wide.at[0])
        relayout(cot.at[layer], cot_o.at[layer + 1], wide.at[1])
    relayout(on_chip.at[0, pl.ds(0, channels)], volume_o.at[rim], wide.at[0])
    relayout(on_chip.at[0, pl.ds(channels, channels)], cot_o.at[rim], wide.at[1])
    edge = 1 + (layers - 1) * (1 - core)

    def products(volume_windows, cot_windows):
        return (
            jnp.dot(forward[...], volume_windows, preferred_element_type=F32),
            jnp.dot(adjoint[...], cot_windows, preferred_element_type=F32),
        )

    for place, layer in enumerate([*range(2, layers), edge]):
        grad_hidden, first_term, second_term = one_layer(
            [volume_o[layer + a] for a in (-1, 0, 1)],
            [cot_o[layer + a] for a in (-1, 0, 1)],
            products,
            columns,
            flat,
        )
        if place < layers - 2:
            grad_o[place] = grad_hidden
        else:
            edge_o[0] = grad_hidden
        if place == 0:
            first_o[...] = first_term
            second_o[...] = second_term
        else:
            first_o[...] += first_term
            second_o[...] += second_term

    layer = 1 + (layers - 1) * core
    for padded in (volume_o, cot_o):
        padded[(layers + 1) * core] = jnp.zeros(padded.shape[1:], BF16)
    part_o[0], part_o[1] = products(
        windows([volume_o[layer + a] for a in (-1, 0, 1)], columns, flat),
        windows([cot_o[layer + a] for a in (-1, 0, 1)], columns, flat),
    )


def pack_first(term):
    half = term.shape[0] // 2
    return term[:, :128], jnp.concatenate([term[:half, 128:], term[half:, 128:]], axis=1)


def pack_second(term):
    half = term.shape[0] // 2
    pieces = [term[:, at : at + 128] for at in range(0, 512, 128)]
    return pieces + [jnp.concatenate([term[:half, 512:], term[half:, 512:]], axis=1)]


def put_rows(dst, pieces):
    at = 0
    for piece in pieces:
        dst[at : at + piece.shape[0], :] = piece
        at += piece.shape[0]


def outer_kernel(
    off_chip,
    volume_p,
    cot_p,
    first_in,
    second_in,
    part,
    forward,
    adjoint,
    edge_o,
    mine_o,
    theirs_o,
    near,
    wide,
):
    layers = volume_p.shape[0] - 2
    channels = off_chip.shape[1] // 2
    rows, columns = off_chip.shape[2:]
    flat = rows * columns
    core = lax.axis_index("gz") & 1
    edge = 1 + (layers - 1) * core
    for kind, padded in enumerate((volume_p, cot_p)):
        rim = near.at[kind, 2 * core]
        zeros = jnp.zeros((channels, columns), BF16)
        rim[:, :columns] = zeros
        rim[:, columns + flat :] = zeros
        relayout(off_chip.at[0, pl.ds(kind * channels, channels)], rim, wide.at[kind])
        near[kind, 1] = padded[edge]
        near[kind, 2 - 2 * core] = padded[edge + 1 - 2 * core]
    depth = 3 * channels
    beyond = pl.ds(pl.multiple_of(2 * depth * core, 128), depth)

    def products(*unused):
        return [
            part[kind]
            + jnp.dot(
                taps[:, beyond],
                jnp.concatenate(
                    [near[kind, 2 * core, :, pl.ds(b * columns, flat)] for b in range(3)], axis=0
                ),
                preferred_element_type=F32,
            )
            for kind, taps in enumerate((forward, adjoint))
        ]

    grad_hidden, first_term, second_term = one_layer(
        [near[0, a] for a in range(3)],
        [near[1, a] for a in range(3)],
        products,
        columns,
        flat,
    )
    edge_o[0] = grad_hidden
    first = pack_first(first_in[...] + first_term)
    second = pack_second(second_in[...] + second_term)

    @pl.when(core == 0)
    def _():
        put_rows(mine_o, first)
        put_rows(theirs_o, second)

    @pl.when(core == 1)
    def _():
        put_rows(mine_o, second)
        put_rows(theirs_o, first)


def volume_kernel(
    on_chip, off_chip, inner, on_edge, off_edge, cot, adjoint, out, padded, wide, buf, out_sem
):
    layers, channels, rows, columns = cot.shape
    flat = rows * columns
    core = lax.axis_index("gz") & 1
    zero_rows(padded, columns)
    middle = slice(columns, columns + flat)
    padded[(1 - core) * (layers + 1), :, middle] = on_chip[0]
    padded[core * (layers + 1), :, middle] = off_chip[0]
    padded[1 + (layers - 1) * (1 - core), :, middle] = on_edge[0]
    padded[1 + (layers - 1) * core, :, middle] = off_edge[0]
    for layer in range(layers - 2):
        padded[layer + 2, :, middle] = inner[layer]
    for layer in range(layers):
        three = jnp.dot(
            adjoint[...],
            windows([padded[layer + a] for a in range(3)], columns, flat),
            preferred_element_type=F32,
        )
        summed = joined(three, -1, columns)
        scratch = wide.at[layer % 2]
        for row in range(rows):
            scratch[pl.ds(row, channels, stride=rows), :] = summed[
                :, row * columns : (row + 1) * columns
            ]
        buf[layer] = (
            cot[layer].astype(F32) + scratch[...].reshape(channels, rows, columns)
        ).astype(BF16)
        pltpu.make_async_copy(buf.at[layer], out.at[layer], out_sem.at[layer]).start()
    for layer in range(layers):
        pltpu.make_async_copy(buf.at[layer], out.at[layer], out_sem.at[layer]).wait()


def unpack_first(src, dst, number, scale):
    channels = dst.shape[1]
    half = 9 * channels // 2
    at = number * channels
    for c in range(2):
        dst[3 * number + c] = (
            src[at : at + channels, c * channels : (c + 1) * channels].astype(F32) * scale
        )
    for low in range(0, channels, channels // 2):
        row = at + low
        part, side = (row, 0) if row < half else (row - half, 1)
        part += 9 * channels
        dst[3 * number + 2, low : low + channels // 2] = (
            src[part : part + channels // 2, side * channels : (side + 1) * channels].astype(F32)
            * scale
        )


def unpack_second(src, dst, number, scale):
    channels = dst.shape[1]
    half = 3 * channels // 2
    place = 8 - number
    for c in range(3):
        if place < 8:
            at = (place // 2) * 3 * channels + c * channels
            side = place % 2
            dst[3 * number + c] = (
                src[at : at + channels, side * channels : (side + 1) * channels].astype(F32)
                * scale
            )
            continue
        for low in range(0, channels, channels // 2):
            row = c * channels + low
            part, side = (row, 0) if row < half else (row - half, 1)
            part += 12 * channels
            dst[3 * number + c, low : low + channels // 2] = (
                src[part : part + channels // 2, side * channels : (side + 1) * channels].astype(
                    F32
                )
                * scale
            )


def unpack_kernel(scale, swap, src, *refs):
    first_o, second_o, buf, sems = refs[-4:]
    core = lax.axis_index("gz") & 1

    def run(unpack, out):
        copies = []
        for depth in range(3):
            for number in range(3 * depth, 3 * depth + 3):
                unpack(src, buf, number, scale)
            part = pl.ds(9 * depth, 9)
            copies.append(pltpu.make_async_copy(buf.at[part], out.at[part], sems.at[depth]))
            copies[-1].start()
        for copy in copies:
            copy.wait()

    @pl.when(core == swap)
    def _():
        run(unpack_first, first_o)

    @pl.when(core == 1 - swap)
    def _():
        run(unpack_second, second_o)


def swapped(array, mask):
    return lax.ppermute(array, "gz", [(i, i ^ mask) for i in range(lax.axis_size("gz"))])


def swapped_apart(array, even, odd):
    masks = (even, odd)
    return lax.ppermute(
        array, "gz", [(i, i ^ masks[i & 1]) for i in range(lax.axis_size("gz"))]
    )


def from_block(arrays):
    diagonal, first, second = arrays
    return [swapped(diagonal, 6), swapped_apart(first, 2, 4), swapped_apart(second, 4, 2)]


def swapped_chips(array):
    pairs = [(i, i + 1) for i in range(1, lax.axis_size("gz") - 1, 2)]
    return lax.ppermute(array, "gz", pairs + [(j, i) for i, j in pairs])


def picked(stack, i):
    return lax.dynamic_index_in_dim(stack, i, 0, keepdims=False)


def quarter_of(mine, theirs):
    quarter = (lax.axis_index("gz") >> 1) & 3
    stack = (mine + swapped(theirs, 1)).reshape(4, -1, *mine.shape[1:])
    core = lax.axis_index("gz") & 1
    sent = [picked(stack, quarter ^ other).astype(BF16) for other in (3, 1 + core, 2 - core)]
    return picked(stack, quarter), sent


def rounded(array):
    top = jnp.max(jnp.abs(array), axis=0, keepdims=True)
    power = jnp.maximum(jnp.ceil(jnp.log2(top)), -100.0)
    return jnp.concatenate(
        [(array * jnp.exp2(14.0 - power)).astype(jnp.float16), power.astype(jnp.float16)]
    )


def widened(coded):
    return coded[:-1].astype(F32) * jnp.exp2(coded[-1:].astype(F32) - 14.0)


def whole_of(total):
    mask = 16
    while mask < lax.axis_size("gz"):
        total = total + swapped(total, mask)
        mask *= 2
    return total.astype(BF16)


def in_order(found, shape):
    quarter = (lax.axis_index("gz") >> 1) & 3
    stack = jnp.stack(found)
    core = lax.axis_index("gz") & 1
    differ = [quarter ^ place for place in range(4)]
    return jnp.stack(
        [
            picked(
                stack,
                jnp.where(d == 0, 0, jnp.where(d == 3, 1, jnp.where(d == 1 + core, 2, 3))),
            )
            for d in differ
        ]
    ).reshape(shape)


def shards(volume, cotangent, first_kernel, second_kernel):
    layers, channels, rows, columns = volume.shape
    flat = rows * columns
    wide = flat + 2 * columns
    devices = lax.axis_size("gz")
    conv_flops = 2 * 27 * channels * channels * flat
    layer_bytes = 2 * channels * flat

    def cost(passes, moved):
        return pl.CostEstimate(
            flops=passes * conv_flops, bytes_accessed=moved * layer_bytes, transcendentals=0
        )

    def params():
        return pltpu.CompilerParams(vmem_limit_bytes=LIMIT)

    shape = jax.ShapeDtypeStruct
    edge = jnp.where(lax.axis_index("gz") & 1 == 0, layers - 1, 0)
    near, far = (
        jnp.concatenate(
            [lax.dynamic_slice_in_dim(field, at, 1) for field in (volume, cotangent)], axis=1
        )
        for at in (edge, layers - 1 - edge)
    )
    off_chip = swapped_chips(far)
    on_chip = swapped(near, 1)

    taps = shape((3 * channels, 9 * channels), BF16)
    layer = shape((1, channels, flat), BF16)
    (
        volume_p,
        cot_p,
        inner,
        on_edge,
        first_in,
        second_in,
        part,
        forward,
        adjoint,
        flipped,
    ) = pl.pallas_call(
        inner_kernel,
        out_shape=(
            shape((layers + 2, channels, wide), BF16),
            shape((layers + 2, channels, wide), BF16),
            shape((layers - 2, channels, flat), BF16),
            layer,
            shape((9 * channels, 3 * channels), F32),
            shape((3 * channels, 9 * channels), F32),
            shape((2, 3 * channels, flat), F32),
            taps,
            taps,
            taps,
        ),
        in_specs=[VM] * 5,
        out_specs=(VM,) * 10,
        scratch_shapes=[pltpu.VMEM((2, channels * rows, columns), F32)],
        compiler_params=params(),
        cost_estimate=cost(4 * (layers - 1), 4 * layers),
        name="inner",
    )(volume, cotangent, on_chip, first_kernel, second_kernel)

    packed = shape((27 * channels * channels // 128, 128), F32)
    off_edge, mine, theirs = pl.pallas_call(
        outer_kernel,
        out_shape=(layer, packed, packed),
        in_specs=[VM] * 8,
        out_specs=(VM,) * 3,
        scratch_shapes=[
            pltpu.VMEM((2, 3, channels, wide), BF16),
            pltpu.VMEM((2, channels * rows, columns), F32),
        ],
        compiler_params=params(),
        cost_estimate=cost(4, 8),
        name="outer",
    )(off_chip, volume_p, cot_p, first_in, second_in, part, forward, adjoint)

    tiles = (packed.shape[0] // 8, 8, 128)
    own, sent = quarter_of(mine.reshape(tiles), theirs.reshape(tiles))
    sent, on_edge = lax.optimization_barrier((sent, on_edge))
    total = own
    for term in from_block(sent):
        total = total + term.astype(F32)
    on_chip_g = swapped(on_edge, 1)
    coded = rounded(total)
    coded, off_edge = lax.optimization_barrier((coded, off_edge))
    off_chip_g = swapped_chips(off_edge)
    total = widened(coded) + widened(swapped(coded, 8))
    total, flipped = lax.optimization_barrier((whole_of(total), flipped))
    grad_volume = pl.pallas_call(
        volume_kernel,
        out_shape=shape(volume.shape, BF16),
        in_specs=[VM] * 7,
        out_specs=ANY,
        scratch_shapes=[
            pltpu.VMEM((layers + 2, channels, wide), BF16),
            pltpu.VMEM((2, channels * rows, columns), F32),
            pltpu.VMEM(volume.shape, BF16),
            pltpu.SemaphoreType.DMA((layers,)),
        ],
        compiler_params=params(),
        cost_estimate=cost(layers, 4 * layers),
        name="volume",
    )(on_chip_g, off_chip_g, inner, on_edge, off_edge, cotangent, flipped)

    found = [total] + from_block([total] * 3)
    found, grad_volume = lax.optimization_barrier((found, grad_volume))
    own = in_order(found, tiles)
    other = swapped(own, 1)
    scale = 1.0 / math.sqrt(layers * devices * flat)
    grads = ()
    for swap, part in enumerate((own, other)):
        grads = pl.pallas_call(
            functools.partial(unpack_kernel, scale, swap),
            out_shape=(shape((27, channels, channels), F32),) * 2,
            in_specs=[VM] + [ANY] * len(grads),
            out_specs=(ANY,) * 2,
            scratch_shapes=[
                pltpu.VMEM((27, channels, channels), F32),
                pltpu.SemaphoreType.DMA((3,)),
            ],
            input_output_aliases={1: 0, 2: 1} if grads else {},
            compiler_params=params(),
            cost_estimate=cost(0, 6),
            name="unpack",
        )(part.reshape(packed.shape), *grads)
    first_grad, second_grad = grads
    return grad_volume, first_grad, second_grad


def solution(mesh):
    placed = (
        P(("groups", "gz"), None, None, None),
        P(("groups", "gz"), None, None, None),
        P(),
        P(),
    )
    return jax.shard_map(
        shards,
        mesh=mesh,
        in_specs=placed,
        out_specs=(
            P(("groups", "gz"), None, None, None),
            P("groups", None, None),
            P("groups", None, None),
        ),
        check_vma=False,
    )
```

```python
import functools
import math

import jax
import jax.numpy as jnp
from jax import lax
from jax.experimental import pallas as pl
from jax.experimental.pallas import tpu as pltpu
from jax.sharding import PartitionSpec as P

F32 = jnp.float32
BF16 = jnp.bfloat16
VM = pl.BlockSpec(memory_space=pltpu.VMEM)
ANY = pl.BlockSpec(memory_space=pl.ANY)
LIMIT = 24 << 20


def relayout(src, dst, wide):
    channels, rows, columns = src.shape
    wide[...] = src[...].astype(F32).reshape(channels * rows, columns)
    for row in range(rows):
        dst[:, (row + 1) * columns : (row + 2) * columns] = wide[
            pl.ds(row, channels, stride=rows), :
        ].astype(BF16)


def zero_rows(padded, columns):
    layers, channels, width = padded.shape
    zeros = jnp.zeros((channels, columns), BF16)
    for layer in range(layers):
        padded[layer, :, :columns] = zeros
        padded[layer, :, width - columns :] = zeros


def windows(three, columns, flat):
    return jnp.concatenate(
        [layer[:, b * columns : b * columns + flat] for layer in three for b in range(3)], axis=0
    )


def shifted(field, step, columns):
    channels, flat = field.shape
    lane = lax.broadcasted_iota(jnp.int32, (channels, columns), 1)
    keep = lane != (0 if step == 1 else columns - 1)
    return jnp.concatenate(
        [
            jnp.where(keep, pltpu.roll(field[:, at : at + columns], step % columns, 1), 0.0)
            for at in range(0, flat, columns)
        ],
        axis=1,
    )


def joined(three, step, columns):
    channels = three.shape[0] // 3
    return (
        three[channels : 2 * channels]
        + shifted(three[:channels], step, columns)
        + shifted(three[2 * channels :], -step, columns)
    )


def column_taps(field, step, columns):
    return jnp.concatenate(
        [
            shifted(field, -step, columns).astype(BF16),
            field.astype(BF16),
            shifted(field, step, columns).astype(BF16),
        ],
        axis=0,
    )


def one_layer(near_volume, near_cot, products, columns, flat):
    volume_windows = windows(near_volume, columns, flat)
    cot_windows = windows(near_cot, columns, flat)
    of_volume, of_cot = products(volume_windows, cot_windows)
    hidden = joined(of_volume, 1, columns)
    back_act = joined(of_cot, -1, columns)
    sigmoid_h = jax.nn.sigmoid(hidden)
    activation = (hidden * sigmoid_h).astype(BF16)
    grad_hidden = (back_act * sigmoid_h * (1.0 + hidden * (1.0 - sigmoid_h))).astype(BF16)
    last = (((1,), (1,)), ((), ()))
    first_term = lax.dot_general(
        volume_windows,
        column_taps(grad_hidden.astype(F32), 1, columns),
        last,
        preferred_element_type=F32,
    )
    second_term = lax.dot_general(
        column_taps(activation.astype(F32), -1, columns),
        cot_windows,
        last,
        preferred_element_type=F32,
    )
    return grad_hidden, first_term, second_term


def forward_taps(taps, out):
    for number in range(9):
        channels = taps.shape[1]
        row = jnp.concatenate([taps[3 * number + c].astype(F32) for c in range(3)], axis=1)
        out[:, number * channels : (number + 1) * channels] = row.T.astype(BF16)


def adjoint_taps(taps, out):
    channels = taps.shape[1]
    for c in range(3):
        out[c * channels : (c + 1) * channels, :] = jnp.concatenate(
            [taps[3 * (8 - number) + c] for number in range(9)], axis=1
        )


def inner_kernel(
    volume,
    cot,
    on_chip,
    first_k,
    second_k,
    volume_o,
    cot_o,
    grad_o,
    edge_o,
    first_o,
    second_o,
    part_o,
    forward,
    adjoint,
    flipped,
    wide,
):
    layers, channels, rows, columns = volume.shape
    flat = rows * columns
    forward_taps(first_k, forward)
    adjoint_taps(second_k, adjoint)
    adjoint_taps(first_k, flipped)
    zero_rows(volume_o, columns)
    zero_rows(cot_o, columns)
    core = lax.axis_index("gz") & 1
    rim = (layers + 1) * (1 - core)
    for layer in range(layers):
        relayout(volume.at[layer], volume_o.at[layer + 1], wide.at[0])
        relayout(cot.at[layer], cot_o.at[layer + 1], wide.at[1])
    relayout(on_chip.at[0, pl.ds(0, channels)], volume_o.at[rim], wide.at[0])
    relayout(on_chip.at[0, pl.ds(channels, channels)], cot_o.at[rim], wide.at[1])
    edge = 1 + (layers - 1) * (1 - core)

    def products(volume_windows, cot_windows):
        return (
            jnp.dot(forward[...], volume_windows, preferred_element_type=F32),
            jnp.dot(adjoint[...], cot_windows, preferred_element_type=F32),
        )

    for place, layer in enumerate([*range(2, layers), edge]):
        grad_hidden, first_term, second_term = one_layer(
            [volume_o[layer + a] for a in (-1, 0, 1)],
            [cot_o[layer + a] for a in (-1, 0, 1)],
            products,
            columns,
            flat,
        )
        if place < layers - 2:
            grad_o[place] = grad_hidden
        else:
            edge_o[0] = grad_hidden
        if place == 0:
            first_o[...] = first_term
            second_o[...] = second_term
        else:
            first_o[...] += first_term
            second_o[...] += second_term

    layer = 1 + (layers - 1) * core
    for padded in (volume_o, cot_o):
        padded[(layers + 1) * core] = jnp.zeros(padded.shape[1:], BF16)
    part_o[0], part_o[1] = products(
        windows([volume_o[layer + a] for a in (-1, 0, 1)], columns, flat),
        windows([cot_o[layer + a] for a in (-1, 0, 1)], columns, flat),
    )


def pack_first(term):
    half = term.shape[0] // 2
    return term[:, :128], jnp.concatenate([term[:half, 128:], term[half:, 128:]], axis=1)


def pack_second(term):
    half = term.shape[0] // 2
    pieces = [term[:, at : at + 128] for at in range(0, 512, 128)]
    return pieces + [jnp.concatenate([term[:half, 512:], term[half:, 512:]], axis=1)]


def put_rows(dst, pieces):
    at = 0
    for piece in pieces:
        dst[at : at + piece.shape[0], :] = piece.astype(dst.dtype)
        at += piece.shape[0]


def outer_kernel(
    off_chip,
    volume_p,
    cot_p,
    first_in,
    second_in,
    part,
    forward,
    adjoint,
    edge_o,
    mine_o,
    theirs_o,
    near,
    wide,
):
    layers = volume_p.shape[0] - 2
    channels = off_chip.shape[1] // 2
    rows, columns = off_chip.shape[2:]
    flat = rows * columns
    core = lax.axis_index("gz") & 1
    edge = 1 + (layers - 1) * core
    for kind, padded in enumerate((volume_p, cot_p)):
        rim = near.at[kind, 2 * core]
        zeros = jnp.zeros((channels, columns), BF16)
        rim[:, :columns] = zeros
        rim[:, columns + flat :] = zeros
        relayout(off_chip.at[0, pl.ds(kind * channels, channels)], rim, wide.at[kind])
        near[kind, 1] = padded[edge]
        near[kind, 2 - 2 * core] = padded[edge + 1 - 2 * core]
    depth = 3 * channels
    beyond = pl.ds(pl.multiple_of(2 * depth * core, 128), depth)

    def products(*unused):
        return [
            part[kind]
            + jnp.dot(
                taps[:, beyond],
                jnp.concatenate(
                    [near[kind, 2 * core, :, pl.ds(b * columns, flat)] for b in range(3)], axis=0
                ),
                preferred_element_type=F32,
            )
            for kind, taps in enumerate((forward, adjoint))
        ]

    grad_hidden, first_term, second_term = one_layer(
        [near[0, a] for a in range(3)],
        [near[1, a] for a in range(3)],
        products,
        columns,
        flat,
    )
    edge_o[0] = grad_hidden
    first = pack_first(first_in[...] + first_term)
    second = pack_second(second_in[...] + second_term)

    @pl.when(core == 0)
    def _():
        put_rows(mine_o, first)
        put_rows(theirs_o, second)

    @pl.when(core == 1)
    def _():
        put_rows(mine_o, second)
        put_rows(theirs_o, first)


def volume_kernel(
    on_chip, off_chip, inner, on_edge, off_edge, cot, adjoint, out, padded, wide, buf, out_sem
):
    layers, channels, rows, columns = cot.shape
    flat = rows * columns
    core = lax.axis_index("gz") & 1
    zero_rows(padded, columns)
    middle = slice(columns, columns + flat)
    padded[(1 - core) * (layers + 1), :, middle] = on_chip[0]
    padded[core * (layers + 1), :, middle] = off_chip[0]
    padded[1 + (layers - 1) * (1 - core), :, middle] = on_edge[0]
    padded[1 + (layers - 1) * core, :, middle] = off_edge[0]
    for layer in range(layers - 2):
        padded[layer + 2, :, middle] = inner[layer]
    for layer in range(layers):
        three = jnp.dot(
            adjoint[...],
            windows([padded[layer + a] for a in range(3)], columns, flat),
            preferred_element_type=F32,
        )
        summed = joined(three, -1, columns)
        scratch = wide.at[layer % 2]
        for row in range(rows):
            scratch[pl.ds(row, channels, stride=rows), :] = summed[
                :, row * columns : (row + 1) * columns
            ]
        buf[layer] = (
            cot[layer].astype(F32) + scratch[...].reshape(channels, rows, columns)
        ).astype(BF16)
        pltpu.make_async_copy(buf.at[layer], out.at[layer], out_sem.at[layer]).start()
    for layer in range(layers):
        pltpu.make_async_copy(buf.at[layer], out.at[layer], out_sem.at[layer]).wait()


def unpack_first(src, dst, number, scale):
    channels = dst.shape[1]
    half = 9 * channels // 2
    at = number * channels
    for c in range(2):
        dst[3 * number + c] = (
            src[at : at + channels, c * channels : (c + 1) * channels].astype(F32) * scale
        )
    for low in range(0, channels, channels // 2):
        row = at + low
        part, side = (row, 0) if row < half else (row - half, 1)
        part += 9 * channels
        dst[3 * number + 2, low : low + channels // 2] = (
            src[part : part + channels // 2, side * channels : (side + 1) * channels].astype(F32)
            * scale
        )


def unpack_second(src, dst, number, scale):
    channels = dst.shape[1]
    half = 3 * channels // 2
    place = 8 - number
    for c in range(3):
        if place < 8:
            at = (place // 2) * 3 * channels + c * channels
            side = place % 2
            dst[3 * number + c] = (
                src[at : at + channels, side * channels : (side + 1) * channels].astype(F32)
                * scale
            )
            continue
        for low in range(0, channels, channels // 2):
            row = c * channels + low
            part, side = (row, 0) if row < half else (row - half, 1)
            part += 12 * channels
            dst[3 * number + c, low : low + channels // 2] = (
                src[part : part + channels // 2, side * channels : (side + 1) * channels].astype(
                    F32
                )
                * scale
            )


def unpack_kernel(scale, swap, src, *refs):
    first_o, second_o, buf, sems = refs[-4:]
    core = lax.axis_index("gz") & 1

    def run(unpack, out):
        copies = []
        for depth in range(3):
            for number in range(3 * depth, 3 * depth + 3):
                unpack(src, buf, number, scale)
            part = pl.ds(9 * depth, 9)
            copies.append(pltpu.make_async_copy(buf.at[part], out.at[part], sems.at[depth]))
            copies[-1].start()
        for copy in copies:
            copy.wait()

    @pl.when(core == swap)
    def _():
        run(unpack_first, first_o)

    @pl.when(core == 1 - swap)
    def _():
        run(unpack_second, second_o)


def swapped(array, mask):
    return lax.ppermute(array, "gz", [(i, i ^ mask) for i in range(lax.axis_size("gz"))])


def swapped_apart(array, even, odd):
    masks = (even, odd)
    return lax.ppermute(
        array, "gz", [(i, i ^ masks[i & 1]) for i in range(lax.axis_size("gz"))]
    )


def from_block(arrays):
    diagonal, first, second = arrays
    return [swapped(diagonal, 6), swapped_apart(first, 2, 4), swapped_apart(second, 4, 2)]


def swapped_chips(array):
    pairs = [(i, i + 1) for i in range(1, lax.axis_size("gz") - 1, 2)]
    return lax.ppermute(array, "gz", pairs + [(j, i) for i, j in pairs])


def picked(stack, i):
    return lax.dynamic_index_in_dim(stack, i, 0, keepdims=False)


def quarter_of(mine, theirs):
    quarter = (lax.axis_index("gz") >> 1) & 3
    stack = (mine + swapped(theirs, 1).astype(F32)).reshape(4, -1, *mine.shape[1:])
    core = lax.axis_index("gz") & 1
    sent = [picked(stack, quarter ^ other).astype(BF16) for other in (3, 1 + core, 2 - core)]
    return picked(stack, quarter), sent


def rounded(array):
    top = jnp.max(jnp.abs(array), axis=0, keepdims=True)
    power = jnp.maximum(jnp.ceil(jnp.log2(top)), -100.0)
    return jnp.concatenate(
        [(array * jnp.exp2(14.0 - power)).astype(jnp.float16), power.astype(jnp.float16)]
    )


def widened(coded):
    return coded[:-1].astype(F32) * jnp.exp2(coded[-1:].astype(F32) - 14.0)


def whole_of(total):
    mask = 16
    while mask < lax.axis_size("gz"):
        total = total + swapped(total, mask)
        mask *= 2
    return total.astype(BF16)


def in_order(found, shape):
    quarter = (lax.axis_index("gz") >> 1) & 3
    stack = jnp.stack(found)
    core = lax.axis_index("gz") & 1
    differ = [quarter ^ place for place in range(4)]
    return jnp.stack(
        [
            picked(
                stack,
                jnp.where(d == 0, 0, jnp.where(d == 3, 1, jnp.where(d == 1 + core, 2, 3))),
            )
            for d in differ
        ]
    ).reshape(shape)


def shards(volume, cotangent, first_kernel, second_kernel):
    layers, channels, rows, columns = volume.shape
    flat = rows * columns
    wide = flat + 2 * columns
    devices = lax.axis_size("gz")
    conv_flops = 2 * 27 * channels * channels * flat
    layer_bytes = 2 * channels * flat

    def cost(passes, moved):
        return pl.CostEstimate(
            flops=passes * conv_flops, bytes_accessed=moved * layer_bytes, transcendentals=0
        )

    def params():
        return pltpu.CompilerParams(vmem_limit_bytes=LIMIT)

    shape = jax.ShapeDtypeStruct
    edge = jnp.where(lax.axis_index("gz") & 1 == 0, layers - 1, 0)
    near, far = (
        jnp.concatenate(
            [lax.dynamic_slice_in_dim(field, at, 1) for field in (volume, cotangent)], axis=1
        )
        for at in (edge, layers - 1 - edge)
    )
    off_chip = swapped_chips(far)
    on_chip = swapped(near, 1)

    taps = shape((3 * channels, 9 * channels), BF16)
    layer = shape((1, channels, flat), BF16)
    (
        volume_p,
        cot_p,
        inner,
        on_edge,
        first_in,
        second_in,
        part,
        forward,
        adjoint,
        flipped,
    ) = pl.pallas_call(
        inner_kernel,
        out_shape=(
            shape((layers + 2, channels, wide), BF16),
            shape((layers + 2, channels, wide), BF16),
            shape((layers - 2, channels, flat), BF16),
            layer,
            shape((9 * channels, 3 * channels), F32),
            shape((3 * channels, 9 * channels), F32),
            shape((2, 3 * channels, flat), F32),
            taps,
            taps,
            taps,
        ),
        in_specs=[VM] * 5,
        out_specs=(VM,) * 10,
        scratch_shapes=[pltpu.VMEM((2, channels * rows, columns), F32)],
        compiler_params=params(),
        cost_estimate=cost(4 * (layers - 1), 4 * layers),
        name="inner",
    )(volume, cotangent, on_chip, first_kernel, second_kernel)

    packed = shape((27 * channels * channels // 128, 128), F32)
    off_edge, mine, theirs = pl.pallas_call(
        outer_kernel,
        out_shape=(layer, packed, shape(packed.shape, BF16)),
        in_specs=[VM] * 8,
        out_specs=(VM,) * 3,
        scratch_shapes=[
            pltpu.VMEM((2, 3, channels, wide), BF16),
            pltpu.VMEM((2, channels * rows, columns), F32),
        ],
        compiler_params=params(),
        cost_estimate=cost(4, 8),
        name="outer",
    )(off_chip, volume_p, cot_p, first_in, second_in, part, forward, adjoint)

    tiles = (packed.shape[0] // 8, 8, 128)
    own, sent = quarter_of(mine.reshape(tiles), theirs.reshape(tiles))
    sent, on_edge = lax.optimization_barrier((sent, on_edge))
    total = own
    for term in from_block(sent):
        total = total + term.astype(F32)
    on_chip_g = swapped(on_edge, 1)
    coded = rounded(total)
    coded, off_edge = lax.optimization_barrier((coded, off_edge))
    off_chip_g = swapped_chips(off_edge)
    total = widened(coded) + widened(swapped(coded, 8))
    total, flipped = lax.optimization_barrier((whole_of(total), flipped))
    grad_volume = pl.pallas_call(
        volume_kernel,
        out_shape=shape(volume.shape, BF16),
        in_specs=[VM] * 7,
        out_specs=ANY,
        scratch_shapes=[
            pltpu.VMEM((layers + 2, channels, wide), BF16),
            pltpu.VMEM((2, channels * rows, columns), F32),
            pltpu.VMEM(volume.shape, BF16),
            pltpu.SemaphoreType.DMA((layers,)),
        ],
        compiler_params=params(),
        cost_estimate=cost(layers, 4 * layers),
        name="volume",
    )(on_chip_g, off_chip_g, inner, on_edge, off_edge, cotangent, flipped)

    found = [total] + from_block([total] * 3)
    found, grad_volume = lax.optimization_barrier((found, grad_volume))
    own = in_order(found, tiles)
    other = swapped(own, 1)
    scale = 1.0 / math.sqrt(layers * devices * flat)
    grads = ()
    for swap, part in enumerate((own, other)):
        grads = pl.pallas_call(
            functools.partial(unpack_kernel, scale, swap),
            out_shape=(shape((27, channels, channels), F32),) * 2,
            in_specs=[VM] + [ANY] * len(grads),
            out_specs=(ANY,) * 2,
            scratch_shapes=[
                pltpu.VMEM((27, channels, channels), F32),
                pltpu.SemaphoreType.DMA((3,)),
            ],
            input_output_aliases={1: 0, 2: 1} if grads else {},
            compiler_params=params(),
            cost_estimate=cost(0, 6),
            name="unpack",
        )(part.reshape(packed.shape), *grads)
    first_grad, second_grad = grads
    return grad_volume, first_grad, second_grad


def solution(mesh):
    placed = (
        P(("groups", "gz"), None, None, None),
        P(("groups", "gz"), None, None, None),
        P(),
        P(),
    )
    return jax.shard_map(
        shards,
        mesh=mesh,
        in_specs=placed,
        out_specs=(
            P(("groups", "gz"), None, None, None),
            P("groups", None, None),
            P("groups", None, None),
        ),
        check_vma=False,
    )
```

```python
import functools
import math

import jax
import jax.numpy as jnp
from jax import lax
from jax.experimental import pallas as pl
from jax.experimental.pallas import tpu as pltpu
from jax.sharding import PartitionSpec as P

F32 = jnp.float32
BF16 = jnp.bfloat16
VM = pl.BlockSpec(memory_space=pltpu.VMEM)
ANY = pl.BlockSpec(memory_space=pl.ANY)
LIMIT = 24 << 20


def relayout(src, dst, wide):
    channels, rows, columns = src.shape
    wide[...] = src[...].astype(F32).reshape(channels * rows, columns)
    for row in range(rows):
        dst[:, (row + 1) * columns : (row + 2) * columns] = wide[
            pl.ds(row, channels, stride=rows), :
        ].astype(BF16)


def zero_rows(padded, columns):
    layers, channels, width = padded.shape
    zeros = jnp.zeros((channels, columns), BF16)
    for layer in range(layers):
        padded[layer, :, :columns] = zeros
        padded[layer, :, width - columns :] = zeros


def windows(three, columns, flat):
    return jnp.concatenate(
        [layer[:, b * columns : b * columns + flat] for layer in three for b in range(3)], axis=0
    )


def shifted(field, step, columns):
    channels, flat = field.shape
    lane = lax.broadcasted_iota(jnp.int32, (channels, columns), 1)
    keep = lane != (0 if step == 1 else columns - 1)
    return jnp.concatenate(
        [
            jnp.where(keep, pltpu.roll(field[:, at : at + columns], step % columns, 1), 0.0)
            for at in range(0, flat, columns)
        ],
        axis=1,
    )


def joined(three, step, columns):
    channels = three.shape[0] // 3
    return (
        three[channels : 2 * channels]
        + shifted(three[:channels], step, columns)
        + shifted(three[2 * channels :], -step, columns)
    )


def column_taps(field, step, columns):
    return jnp.concatenate(
        [
            shifted(field, -step, columns).astype(BF16),
            field.astype(BF16),
            shifted(field, step, columns).astype(BF16),
        ],
        axis=0,
    )


def one_layer(near_volume, near_cot, products, columns, flat):
    volume_windows = windows(near_volume, columns, flat)
    cot_windows = windows(near_cot, columns, flat)
    of_volume, of_cot = products(volume_windows, cot_windows)
    hidden = joined(of_volume, 1, columns)
    back_act = joined(of_cot, -1, columns)
    sigmoid_h = jax.nn.sigmoid(hidden)
    activation = (hidden * sigmoid_h).astype(BF16)
    grad_hidden = (back_act * sigmoid_h * (1.0 + hidden * (1.0 - sigmoid_h))).astype(BF16)
    last = (((1,), (1,)), ((), ()))
    first_term = lax.dot_general(
        volume_windows,
        column_taps(grad_hidden.astype(F32), 1, columns),
        last,
        preferred_element_type=F32,
    )
    second_term = lax.dot_general(
        cot_windows,
        column_taps(activation.astype(F32), -1, columns),
        last,
        preferred_element_type=F32,
    )
    return grad_hidden, first_term, second_term


def forward_taps(taps, out):
    for number in range(9):
        channels = taps.shape[1]
        row = jnp.concatenate([taps[3 * number + c].astype(F32) for c in range(3)], axis=1)
        out[:, number * channels : (number + 1) * channels] = row.T.astype(BF16)


def adjoint_taps(taps, out):
    channels = taps.shape[1]
    for c in range(3):
        out[c * channels : (c + 1) * channels, :] = jnp.concatenate(
            [taps[3 * (8 - number) + c] for number in range(9)], axis=1
        )


def inner_kernel(
    volume,
    cot,
    on_chip,
    first_k,
    second_k,
    volume_o,
    cot_o,
    grad_o,
    edge_o,
    first_o,
    second_o,
    part_o,
    forward,
    adjoint,
    flipped,
    wide,
):
    layers, channels, rows, columns = volume.shape
    flat = rows * columns
    forward_taps(first_k, forward)
    adjoint_taps(second_k, adjoint)
    adjoint_taps(first_k, flipped)
    zero_rows(volume_o, columns)
    zero_rows(cot_o, columns)
    core = lax.axis_index("gz") & 1
    rim = (layers + 1) * (1 - core)
    for layer in range(layers):
        relayout(volume.at[layer], volume_o.at[layer + 1], wide.at[0])
        relayout(cot.at[layer], cot_o.at[layer + 1], wide.at[1])
    relayout(on_chip.at[0, pl.ds(0, channels)], volume_o.at[rim], wide.at[0])
    relayout(on_chip.at[0, pl.ds(channels, channels)], cot_o.at[rim], wide.at[1])
    edge = 1 + (layers - 1) * (1 - core)

    def products(volume_windows, cot_windows):
        return (
            jnp.dot(forward[...], volume_windows, preferred_element_type=F32),
            jnp.dot(adjoint[...], cot_windows, preferred_element_type=F32),
        )

    for place, layer in enumerate([*range(2, layers), edge]):
        grad_hidden, first_term, second_term = one_layer(
            [volume_o[layer + a] for a in (-1, 0, 1)],
            [cot_o[layer + a] for a in (-1, 0, 1)],
            products,
            columns,
            flat,
        )
        if place < layers - 2:
            grad_o[place] = grad_hidden
        else:
            edge_o[0] = grad_hidden
        if place == 0:
            first_o[...] = first_term
            second_o[...] = second_term
        else:
            first_o[...] += first_term
            second_o[...] += second_term

    layer = 1 + (layers - 1) * core
    for padded in (volume_o, cot_o):
        padded[(layers + 1) * core] = jnp.zeros(padded.shape[1:], BF16)
    part_o[0], part_o[1] = products(
        windows([volume_o[layer + a] for a in (-1, 0, 1)], columns, flat),
        windows([cot_o[layer + a] for a in (-1, 0, 1)], columns, flat),
    )


def pack_first(term):
    half = term.shape[0] // 2
    return term[:, :128], jnp.concatenate([term[:half, 128:], term[half:, 128:]], axis=1)


def pack_second(term):
    half = term.shape[0] // 2
    pieces = [term[:, at : at + 128] for at in range(0, 512, 128)]
    return pieces + [jnp.concatenate([term[:half, 512:], term[half:, 512:]], axis=1)]


def put_rows(dst, pieces):
    at = 0
    for piece in pieces:
        dst[at : at + piece.shape[0], :] = piece
        at += piece.shape[0]


def outer_kernel(
    off_chip,
    volume_p,
    cot_p,
    first_in,
    second_in,
    part,
    forward,
    adjoint,
    edge_o,
    mine_o,
    theirs_o,
    near,
    wide,
):
    layers = volume_p.shape[0] - 2
    channels = off_chip.shape[1] // 2
    rows, columns = off_chip.shape[2:]
    flat = rows * columns
    core = lax.axis_index("gz") & 1
    edge = 1 + (layers - 1) * core
    for kind, padded in enumerate((volume_p, cot_p)):
        rim = near.at[kind, 2 * core]
        zeros = jnp.zeros((channels, columns), BF16)
        rim[:, :columns] = zeros
        rim[:, columns + flat :] = zeros
        relayout(off_chip.at[0, pl.ds(kind * channels, channels)], rim, wide.at[kind])
        near[kind, 1] = padded[edge]
        near[kind, 2 - 2 * core] = padded[edge + 1 - 2 * core]
    depth = 3 * channels
    beyond = pl.ds(pl.multiple_of(2 * depth * core, 128), depth)

    def products(*unused):
        return [
            part[kind]
            + jnp.dot(
                taps[:, beyond],
                jnp.concatenate(
                    [near[kind, 2 * core, :, pl.ds(b * columns, flat)] for b in range(3)], axis=0
                ),
                preferred_element_type=F32,
            )
            for kind, taps in enumerate((forward, adjoint))
        ]

    grad_hidden, first_term, second_term = one_layer(
        [near[0, a] for a in range(3)],
        [near[1, a] for a in range(3)],
        products,
        columns,
        flat,
    )
    edge_o[0] = grad_hidden
    first = pack_first(first_in[...] + first_term)
    second = pack_second((second_in[...] + second_term).T)

    @pl.when(core == 0)
    def _():
        put_rows(mine_o, first)
        put_rows(theirs_o, second)

    @pl.when(core == 1)
    def _():
        put_rows(mine_o, second)
        put_rows(theirs_o, first)


def volume_kernel(
    on_chip, off_chip, inner, on_edge, off_edge, cot, adjoint, out, padded, wide, buf, out_sem
):
    layers, channels, rows, columns = cot.shape
    flat = rows * columns
    core = lax.axis_index("gz") & 1
    zero_rows(padded, columns)
    middle = slice(columns, columns + flat)
    padded[(1 - core) * (layers + 1), :, middle] = on_chip[0]
    padded[core * (layers + 1), :, middle] = off_chip[0]
    padded[1 + (layers - 1) * (1 - core), :, middle] = on_edge[0]
    padded[1 + (layers - 1) * core, :, middle] = off_edge[0]
    for layer in range(layers - 2):
        padded[layer + 2, :, middle] = inner[layer]
    for layer in range(layers):
        three = jnp.dot(
            adjoint[...],
            windows([padded[layer + a] for a in range(3)], columns, flat),
            preferred_element_type=F32,
        )
        summed = joined(three, -1, columns)
        scratch = wide.at[layer % 2]
        for row in range(rows):
            scratch[pl.ds(row, channels, stride=rows), :] = summed[
                :, row * columns : (row + 1) * columns
            ]
        buf[layer] = (
            cot[layer].astype(F32) + scratch[...].reshape(channels, rows, columns)
        ).astype(BF16)
        pltpu.make_async_copy(buf.at[layer], out.at[layer], out_sem.at[layer]).start()
    for layer in range(layers):
        pltpu.make_async_copy(buf.at[layer], out.at[layer], out_sem.at[layer]).wait()


def unpack_first(src, dst, number, scale):
    channels = dst.shape[1]
    half = 9 * channels // 2
    at = number * channels
    for c in range(2):
        dst[3 * number + c] = (
            src[at : at + channels, c * channels : (c + 1) * channels].astype(F32) * scale
        )
    for low in range(0, channels, channels // 2):
        row = at + low
        part, side = (row, 0) if row < half else (row - half, 1)
        part += 9 * channels
        dst[3 * number + 2, low : low + channels // 2] = (
            src[part : part + channels // 2, side * channels : (side + 1) * channels].astype(F32)
            * scale
        )


def unpack_second(src, dst, number, scale):
    channels = dst.shape[1]
    half = 3 * channels // 2
    place = 8 - number
    for c in range(3):
        if place < 8:
            at = (place // 2) * 3 * channels + c * channels
            side = place % 2
            dst[3 * number + c] = (
                src[at : at + channels, side * channels : (side + 1) * channels].astype(F32)
                * scale
            )
            continue
        for low in range(0, channels, channels // 2):
            row = c * channels + low
            part, side = (row, 0) if row < half else (row - half, 1)
            part += 12 * channels
            dst[3 * number + c, low : low + channels // 2] = (
                src[part : part + channels // 2, side * channels : (side + 1) * channels].astype(
                    F32
                )
                * scale
            )


def unpack_kernel(scale, swap, src, *refs):
    first_o, second_o, buf, sems = refs[-4:]
    core = lax.axis_index("gz") & 1

    def run(unpack, out):
        copies = []
        for depth in range(3):
            for number in range(3 * depth, 3 * depth + 3):
                unpack(src, buf, number, scale)
            part = pl.ds(9 * depth, 9)
            copies.append(pltpu.make_async_copy(buf.at[part], out.at[part], sems.at[depth]))
            copies[-1].start()
        for copy in copies:
            copy.wait()

    @pl.when(core == swap)
    def _():
        run(unpack_first, first_o)

    @pl.when(core == 1 - swap)
    def _():
        run(unpack_second, second_o)


def swapped(array, mask):
    return lax.ppermute(array, "gz", [(i, i ^ mask) for i in range(lax.axis_size("gz"))])


def swapped_apart(array, even, odd):
    masks = (even, odd)
    return lax.ppermute(
        array, "gz", [(i, i ^ masks[i & 1]) for i in range(lax.axis_size("gz"))]
    )


def from_block(arrays):
    diagonal, first, second = arrays
    return [swapped(diagonal, 6), swapped_apart(first, 2, 4), swapped_apart(second, 4, 2)]


def swapped_chips(array):
    pairs = [(i, i + 1) for i in range(1, lax.axis_size("gz") - 1, 2)]
    return lax.ppermute(array, "gz", pairs + [(j, i) for i, j in pairs])


def picked(stack, i):
    return lax.dynamic_index_in_dim(stack, i, 0, keepdims=False)


def quarter_of(mine, theirs):
    quarter = (lax.axis_index("gz") >> 1) & 3
    stack = (mine + swapped(theirs, 1)).reshape(4, -1, *mine.shape[1:])
    core = lax.axis_index("gz") & 1
    sent = [picked(stack, quarter ^ other).astype(BF16) for other in (3, 1 + core, 2 - core)]
    return picked(stack, quarter), sent


def rounded(array):
    top = jnp.max(jnp.abs(array), axis=0, keepdims=True)
    power = jnp.maximum(jnp.ceil(jnp.log2(top)), -100.0)
    return jnp.concatenate(
        [(array * jnp.exp2(14.0 - power)).astype(jnp.float16), power.astype(jnp.float16)]
    )


def widened(coded):
    return coded[:-1].astype(F32) * jnp.exp2(coded[-1:].astype(F32) - 14.0)


def whole_of(total):
    mask = 16
    while mask < lax.axis_size("gz"):
        total = total + swapped(total, mask)
        mask *= 2
    return total.astype(BF16)


def in_order(found, shape):
    quarter = (lax.axis_index("gz") >> 1) & 3
    stack = jnp.stack(found)
    core = lax.axis_index("gz") & 1
    differ = [quarter ^ place for place in range(4)]
    return jnp.stack(
        [
            picked(
                stack,
                jnp.where(d == 0, 0, jnp.where(d == 3, 1, jnp.where(d == 1 + core, 2, 3))),
            )
            for d in differ
        ]
    ).reshape(shape)


def shards(volume, cotangent, first_kernel, second_kernel):
    layers, channels, rows, columns = volume.shape
    flat = rows * columns
    wide = flat + 2 * columns
    devices = lax.axis_size("gz")
    conv_flops = 2 * 27 * channels * channels * flat
    layer_bytes = 2 * channels * flat

    def cost(passes, moved):
        return pl.CostEstimate(
            flops=passes * conv_flops, bytes_accessed=moved * layer_bytes, transcendentals=0
        )

    def params():
        return pltpu.CompilerParams(vmem_limit_bytes=LIMIT)

    shape = jax.ShapeDtypeStruct
    edge = jnp.where(lax.axis_index("gz") & 1 == 0, layers - 1, 0)
    near, far = (
        jnp.concatenate(
            [lax.dynamic_slice_in_dim(field, at, 1) for field in (volume, cotangent)], axis=1
        )
        for at in (edge, layers - 1 - edge)
    )
    off_chip = swapped_chips(far)
    on_chip = swapped(near, 1)

    taps = shape((3 * channels, 9 * channels), BF16)
    layer = shape((1, channels, flat), BF16)
    (
        volume_p,
        cot_p,
        inner,
        on_edge,
        first_in,
        second_in,
        part,
        forward,
        adjoint,
        flipped,
    ) = pl.pallas_call(
        inner_kernel,
        out_shape=(
            shape((layers + 2, channels, wide), BF16),
            shape((layers + 2, channels, wide), BF16),
            shape((layers - 2, channels, flat), BF16),
            layer,
            shape((9 * channels, 3 * channels), F32),
            shape((9 * channels, 3 * channels), F32),
            shape((2, 3 * channels, flat), F32),
            taps,
            taps,
            taps,
        ),
        in_specs=[VM] * 5,
        out_specs=(VM,) * 10,
        scratch_shapes=[pltpu.VMEM((2, channels * rows, columns), F32)],
        compiler_params=params(),
        cost_estimate=cost(4 * (layers - 1), 4 * layers),
        name="inner",
    )(volume, cotangent, on_chip, first_kernel, second_kernel)

    packed = shape((27 * channels * channels // 128, 128), F32)
    off_edge, mine, theirs = pl.pallas_call(
        outer_kernel,
        out_shape=(layer, packed, packed),
        in_specs=[VM] * 8,
        out_specs=(VM,) * 3,
        scratch_shapes=[
            pltpu.VMEM((2, 3, channels, wide), BF16),
            pltpu.VMEM((2, channels * rows, columns), F32),
        ],
        compiler_params=params(),
        cost_estimate=cost(4, 8),
        name="outer",
    )(off_chip, volume_p, cot_p, first_in, second_in, part, forward, adjoint)

    tiles = (packed.shape[0] // 8, 8, 128)
    own, sent = quarter_of(mine.reshape(tiles), theirs.reshape(tiles))
    sent, on_edge = lax.optimization_barrier((sent, on_edge))
    total = own
    for term in from_block(sent):
        total = total + term.astype(F32)
    on_chip_g = swapped(on_edge, 1)
    coded = rounded(total)
    coded, off_edge = lax.optimization_barrier((coded, off_edge))
    off_chip_g = swapped_chips(off_edge)
    total = widened(coded) + widened(swapped(coded, 8))
    total, flipped = lax.optimization_barrier((whole_of(total), flipped))
    grad_volume = pl.pallas_call(
        volume_kernel,
        out_shape=shape(volume.shape, BF16),
        in_specs=[VM] * 7,
        out_specs=ANY,
        scratch_shapes=[
            pltpu.VMEM((layers + 2, channels, wide), BF16),
            pltpu.VMEM((2, channels * rows, columns), F32),
            pltpu.VMEM(volume.shape, BF16),
            pltpu.SemaphoreType.DMA((layers,)),
        ],
        compiler_params=params(),
        cost_estimate=cost(layers, 4 * layers),
        name="volume",
    )(on_chip_g, off_chip_g, inner, on_edge, off_edge, cotangent, flipped)

    found = [total] + from_block([total] * 3)
    found, grad_volume = lax.optimization_barrier((found, grad_volume))
    own = in_order(found, tiles)
    other = swapped(own, 1)
    scale = 1.0 / math.sqrt(layers * devices * flat)
    grads = ()
    for swap, part in enumerate((own, other)):
        grads = pl.pallas_call(
            functools.partial(unpack_kernel, scale, swap),
            out_shape=(shape((27, channels, channels), F32),) * 2,
            in_specs=[VM] + [ANY] * len(grads),
            out_specs=(ANY,) * 2,
            scratch_shapes=[
                pltpu.VMEM((27, channels, channels), F32),
                pltpu.SemaphoreType.DMA((3,)),
            ],
            input_output_aliases={1: 0, 2: 1} if grads else {},
            compiler_params=params(),
            cost_estimate=cost(0, 6),
            name="unpack",
        )(part.reshape(packed.shape), *grads)
    first_grad, second_grad = grads
    return grad_volume, first_grad, second_grad


def solution(mesh):
    placed = (
        P(("groups", "gz"), None, None, None),
        P(("groups", "gz"), None, None, None),
        P(),
        P(),
    )
    return jax.shard_map(
        shards,
        mesh=mesh,
        in_specs=placed,
        out_specs=(
            P(("groups", "gz"), None, None, None),
            P("groups", None, None),
            P("groups", None, None),
        ),
        check_vma=False,
    )
```
